32 devices in a mesh: ctx: 8 (over z, y), exp: 4 (over x, core).
Axes of the slice: x: 2, y: 2, z: 4, core: 2. Of those that a mesh axis runs over, the one named last changes fastest.
Arguments:
- frames: bfloat16 [4, 768, 2048], P('exp', 'ctx'), may hold values from -6 to 6
- queries: bfloat16 [4, 768, 2048], P('exp', 'ctx'), may hold values from -8 to 8
- keys: bfloat16 [4, 768, 2048], P('exp', 'ctx'), may hold values from -8 to 8
- values: bfloat16 [4, 768, 2048], P('exp', 'ctx'), may hold values from -6 to 6
- expert_ids: int32 [4, 768, 2], P('exp', 'ctx'), may hold values from 0 to 7, all different within a row; in each aligned block of 96 rows (0 to 95, 96 to 191, ..., all dimensions but the last counted through in order) at most 48 rows name the same one
- gate_weights: float32 [4, 768, 2], P('exp', 'ctx'), may hold values from 0.2 to 1
- w_in: bfloat16 [8, 2048, 8192], P('exp', None, 'ctx'), may hold values from -0.125 to 0.125
- w_out: bfloat16 [8, 8192, 2048], P('exp', 'ctx'), may hold values from -0.0625 to 0.0625
Outputs:
- layer_out: bfloat16 [4, 768, 2048], P('exp', 'ctx')
The draws below stay inside these ranges and needn't reach their ends.
Inputs may be any that keep to these rules, and one draw needn't show every extreme that they name: `expert_ids`: each row names two different experts; within the rows of one device no expert is named by more than 48 rows, a bound that some block reaches.
All inputs are finite; a program needn't handle non-finite values.
Results may differ from the reference program's by a relative error of at most 0.013.
Values may be sent and summed in bfloat16 or wider, within the bound.
No kernel may reach another device: no remote copies, remote signals or barrier semaphores. Data moves between devices by JAX's collectives and lax.ppermute only.
A program may use at most 192 MiB of HBM per device.

```python
import math
import jax
import jax.numpy as jnp
import numpy as np
from jax import lax

D = 2048
HEADS = 16
HD = 128
FF = 8192
TOK_DEV = 96
EXPERTS = 8
SEQS = 4
LEN = 768
FFD = 1024
CAP = 48
N_CTX = 8
N_EXP = 4


def draw_queries(key, part):
    drawn = 1.4 * jax.random.normal(jax.random.fold_in(key, 11), (SEQS, LEN, HEADS * HD), jnp.float32)
    return jnp.clip(drawn, -8.0, 8.0).astype(jnp.bfloat16)


def draw_keys(key, part):
    drawn = 1.4 * jax.random.normal(jax.random.fold_in(key, 13), (SEQS, LEN, HEADS * HD), jnp.float32)
    return jnp.clip(drawn, -8.0, 8.0).astype(jnp.bfloat16)


def block_scale(key, shape, cuts, least, top_value):
    gain, own = 1.0, jax.random.fold_in(key, 6)
    for dim, shards_of in cuts:
        steps = jnp.exp(jax.random.uniform(jax.random.fold_in(own, dim), (shards_of,), jnp.float32, least / len(cuts), top_value / len(cuts)))
        gain = gain * jnp.repeat(steps, shape[dim] // shards_of).reshape([-1 if axis == dim else 1 for axis in range(len(shape))])
    return gain


def shared_out(own_key, own, number, rows, count, top, most, slope):
    sequence = jax.random.permutation(own_key, count)
    heavy_load, common = load_shares(count, rows * top, most, slope, True), load_shares(count, rows * top, most, slope, False)
    places = jnp.arange(count)

    def named(sizes, rotation):
        used = int((sizes > 0).sum())
        fixed = max(1, used // 4)
        moved = fixed + (places - fixed + rotation * (used - fixed)) % max(1, count - fixed)
        return jnp.zeros((count,), jnp.int32).at[sequence[jnp.where(places < fixed, places, moved)]].set(jnp.asarray(sizes, jnp.int32))

    sizes = jnp.where(number % 4 == 0, named(heavy_load, number // 4), named(common, number - number // 4 - 1))
    mixed = jax.random.permutation(jax.random.fold_in(own, 3), count)
    source_of, receiver = mixed[0:count // 2 * 2:2], mixed[1:count // 2 * 2:2]
    slack = jnp.minimum(sizes[source_of] - 1, most - sizes[receiver]) // 2
    slack = jnp.where((source_of == sequence[0]) | (receiver == sequence[0]) | (sizes[receiver] == 0), 0, jnp.maximum(slack, 0))
    moved = jax.random.randint(jax.random.fold_in(own, 4), (count // 2,), 0, 1 << 20) % (slack + 1)
    sizes = sizes.at[source_of].add(-moved).at[receiver].add(moved)
    labels = jnp.searchsorted(jnp.cumsum(sizes), jnp.arange(rows * top), side="right").astype(jnp.int32)
    table = labels.reshape(top, rows).T
    table = table[jax.random.permutation(jax.random.fold_in(own, 1), rows)]
    rotation = jax.random.randint(jax.random.fold_in(own, 2), (rows, 1), 0, top)
    return jnp.take_along_axis(table, (jnp.arange(top)[None, :] + rotation) % top, axis=1)


def load_shares(number_of, total, most, lean, full):
    portions = [(1 << 20) // math.isqrt(standing ** lean) + 1 for standing in range(1, number_of + 1)]
    largest = most if full else min(most, max(-(-total // number_of), total * portions[0] // sum(portions)))
    least = 1 if total - largest >= number_of - 1 else 0
    holding, rest = [largest] + [least] * (number_of - 1), total - largest - least * (number_of - 1)
    while rest > 0:
        movable = [i for i in range(1, number_of) if holding[i] < largest] or [i for i in range(1, number_of) if holding[i] < most]
        pool, left = sum([portions[i] for i in movable]), rest
        for i in movable:
            more = min(most - holding[i], max(1, left * portions[i] // pool), rest)
            holding[i] = holding[i] + more
            rest = rest - more
    return np.array(holding)


def normal_values(stream_key, dims, spread, most, cuts=(), kind=jnp.bfloat16):
    level = block_scale(stream_key, dims, cuts, -0.22, 0.18) if cuts else 1.0
    entries = jax.random.normal(stream_key, dims, jnp.float32) * spread * level
    return jnp.minimum(jnp.maximum(entries, -most), most).astype(kind)


def setup_inputs(seed: int = 0) -> dict:
    seeds = jax.random.split(jax.random.key(seed), 9)
    frames = normal_values(seeds[0], (SEQS, LEN, D), 1.0, 6.0, ((0, 4), (1, 8)))
    queries = draw_queries(jax.random.fold_in(seeds[8], 71), 0)
    keys = draw_keys(jax.random.fold_in(seeds[8], 71), 0)
    values = normal_values(seeds[3], (SEQS, LEN, D), 1.0, 6.0, ((0, 4), (1, 8)))
    expert_ids_keys = jax.random.split(jax.random.fold_in(seeds[4], 1), SEQS * LEN // TOK_DEV)
    expert_ids_turns = jax.random.permutation(jax.random.fold_in(seeds[4], 3), SEQS * LEN // TOK_DEV)
    expert_ids = jax.vmap(lambda own, number: shared_out(jax.random.fold_in(seeds[4], 2), own, number, TOK_DEV, EXPERTS, 2, CAP, 2))(expert_ids_keys, expert_ids_turns).reshape((SEQS, LEN, 2))
    gate_weights = jnp.clip(0.2 + 0.8 * jax.random.uniform(seeds[5], (SEQS, LEN, 2), jnp.float32) ** block_scale(seeds[5], (SEQS, LEN, 2), ((0, 4), (1, 8)), -0.2, 0.2), 0.2, 1.0)
    w_in = normal_values(seeds[6], (EXPERTS, D, FF), D ** -0.5, 0.125, ((0, 4), (2, 8)))
    w_out = normal_values(seeds[7], (EXPERTS, FF, D), FF ** -0.5, 0.0625, ((0, 4), (1, 8)))
    return dict(frames=frames, queries=queries, keys=keys, values=values, expert_ids=expert_ids, gate_weights=gate_weights, w_in=w_in, w_out=w_out)


EPSILON = 1e-05

def gelu_tanh(values_in):
    return jax.nn.gelu(values_in, approximate=True)

def attend_sequence(triple):
    queries_seq, keys_seq, values_seq = triple
    factor = 1.0 / math.sqrt(HD)
    query_heads = queries_seq.reshape(LEN, HEADS, HD).astype(jnp.float32)
    key_heads = keys_seq.reshape(LEN, HEADS, HD).astype(jnp.float32)
    value_heads = values_seq.reshape(LEN, HEADS, HD).astype(jnp.float32)
    scores = jnp.einsum('qhd,khd->hqk', query_heads, key_heads) * factor
    top_score = lax.optimization_barrier(jnp.max(scores, axis=-1, keepdims=True))
    weights_raw = jnp.exp(scores - top_score)
    totals = lax.optimization_barrier(jnp.sum(weights_raw, axis=-1))
    rounded = lax.optimization_barrier(weights_raw.astype(jnp.bfloat16)).astype(jnp.float32)
    mixed_out = jnp.einsum('hqk,khd->hqd', rounded, value_heads) / totals[..., None]
    return jnp.transpose(mixed_out, (1, 0, 2)).reshape(LEN, HEADS * HD)

def reference(frames, queries, keys, values, expert_ids, gate_weights, w_in, w_out):
    attended = lax.map(attend_sequence, (queries, keys, values))
    hidden_state = (frames.astype(jnp.float32) + attended).astype(jnp.bfloat16)
    hidden_f = hidden_state.astype(jnp.float32)
    normed = (hidden_f * lax.rsqrt(lax.optimization_barrier(jnp.mean(hidden_f * hidden_f, axis=-1, keepdims=True)) + EPSILON)).astype(jnp.bfloat16)
    flat_tokens = normed.reshape(SEQS * LEN, D)
    slot_ids = expert_ids.reshape(-1).astype(jnp.int32)
    row_cap = CAP * N_CTX * N_EXP

    def per_expert(collected, stacked):
        expert_num, first_w, second_w = stacked
        matched = slot_ids == expert_num
        order_idx = jnp.argsort(jnp.where(matched, 0, 1).astype(jnp.int32), stable=True)[:row_cap].astype(jnp.int32)
        usable = matched[order_idx]
        rows_in = flat_tokens[order_idx // 2]
        inner_act = gelu_tanh(jnp.dot(rows_in, first_w, preferred_element_type=jnp.float32)).astype(jnp.bfloat16)
        pieces = jnp.einsum('rcf,cfd->crd', inner_act.reshape(row_cap, N_CTX, FFD).astype(jnp.float32), second_w.reshape(N_CTX, FFD, D).astype(jnp.float32))
        rounded = lax.optimization_barrier(pieces.astype(jnp.bfloat16)).astype(jnp.float32)
        expert_out = lax.optimization_barrier(lax.optimization_barrier(jnp.sum(rounded, axis=0)).astype(jnp.bfloat16)).astype(jnp.float32)
        collected = collected.at[order_idx].add(jnp.where(usable[:, None], expert_out, jnp.zeros_like(expert_out)))
        return (collected, None)
    initial = jnp.zeros((SEQS * LEN * 2, D), jnp.float32)
    collected, unused = lax.scan(per_expert, initial, (jnp.arange(EXPERTS, dtype=jnp.int32), w_in, w_out))
    slot_out = collected.reshape(SEQS, LEN, 2, D)
    layer_out = hidden_f + gate_weights[..., 0:1] * slot_out[:, :, 0] + gate_weights[..., 1:2] * slot_out[:, :, 1]
    return layer_out.astype(jnp.bfloat16)
```

```python
import functools
import math

import jax
import jax.numpy as jnp
from jax import lax
from jax.experimental import pallas as pl
from jax.experimental.pallas import tpu as pltpu
from jax.sharding import PartitionSpec as P

HEADS = 16
HD = 128


EPSILON = 1e-05


def gelu_tanh(values_in):
    return jax.nn.gelu(values_in, approximate=True)


def expert_partial(gathered, live_flags, first_w, second_w):
    total_rows = gathered.shape[0]
    out_width = second_w.shape[1]
    padded_rows = -(-total_rows // 128) * 128
    position = jnp.cumsum(live_flags) - 1
    live_count = jnp.sum(live_flags)
    target = jnp.where(live_flags > 0, position, padded_rows)
    order_idx = (
        jnp.zeros((padded_rows,), jnp.int32)
        .at[target]
        .set(jnp.arange(total_rows, dtype=jnp.int32), mode="drop")
    )
    block_count = (live_count + 127) // 128

    def one_block(block_num, packed):
        picked = lax.dynamic_slice_in_dim(order_idx, block_num * 128, 128)
        inputs = jnp.take(gathered, picked, axis=0)
        inner_act = gelu_tanh(jnp.dot(inputs, first_w, preferred_element_type=jnp.float32)).astype(
            jnp.bfloat16
        )
        output = jnp.dot(inner_act, second_w, preferred_element_type=jnp.float32).astype(
            jnp.bfloat16
        )
        return lax.dynamic_update_slice_in_dim(packed, output, block_num * 128, 0)

    packed = lax.fori_loop(
        0, block_count, one_block, jnp.zeros((padded_rows, out_width), jnp.bfloat16)
    )
    back_idx = jnp.where(live_flags > 0, position, 0).astype(jnp.int32)
    unpacked = jnp.take(packed, back_idx, axis=0)
    return jnp.where((live_flags > 0)[:, None], unpacked, jnp.zeros_like(unpacked))


def routed_ffn(hidden_f, normed, expert_ids, gate_weights, w_in, w_out):
    tok_count, model_width = normed.shape
    slot_ids = expert_ids[0].reshape(-1)
    slot_count = slot_ids.shape[0]
    exp_local = w_in.shape[0]
    num_experts = exp_local * lax.axis_size("exp")
    capacity = 2 * (slot_count // num_experts)
    onehot = (slot_ids[:, None] == jnp.arange(num_experts, dtype=jnp.int32)[None, :]).astype(
        jnp.int32
    )
    slot_rank = jnp.sum((jnp.cumsum(onehot, axis=0) - onehot) * onehot, axis=1)
    target = slot_ids * capacity + slot_rank
    send_matrix = (
        jnp.arange(num_experts * capacity, dtype=jnp.int32)[:, None] == target[None, :]
    ).astype(jnp.int32)
    token_matrix = send_matrix.reshape(num_experts * capacity, tok_count, 2).sum(-1)
    outgoing = jnp.dot(
        token_matrix.astype(jnp.bfloat16), normed, preferred_element_type=jnp.float32
    ).astype(jnp.bfloat16)
    outgoing = outgoing.reshape(num_experts, capacity, model_width)
    occupied = jnp.sum(send_matrix, axis=1).reshape(num_experts, capacity)
    arrived, arrived_flags = (
        lax.all_to_all(outgoing, "exp", split_axis=0, concat_axis=1, tiled=True),
        lax.all_to_all(occupied, "exp", split_axis=0, concat_axis=1, tiled=True),
    )
    gathered, gathered_flags = (
        lax.all_gather(arrived, "ctx", axis=1, tiled=True),
        lax.all_gather(arrived_flags, "ctx", axis=1, tiled=True),
    )
    summed_list = []
    for local_num in range(exp_local):
        partial_value = expert_partial(
            gathered[local_num], gathered_flags[local_num], w_in[local_num], w_out[local_num]
        )
        summed_list.append(
            lax.psum_scatter(partial_value, "ctx", scatter_dimension=0, tiled=True)
            .astype(jnp.float32)
            .astype(jnp.bfloat16)
        )
    summed = jnp.stack(summed_list)
    returned = lax.all_to_all(summed, "exp", split_axis=1, concat_axis=0, tiled=True)
    slot_out = jnp.dot(
        send_matrix.T.astype(jnp.bfloat16),
        returned.reshape(num_experts * capacity, model_width),
        preferred_element_type=jnp.float32,
    )
    tok_out = slot_out.reshape(tok_count, 2, model_width)
    gates = gate_weights[0]
    return hidden_f + gates[:, 0:1] * tok_out[:, 0] + gates[:, 1:2] * tok_out[:, 1]


def attend_kernel(q_ref, k_ref, v_ref, o_ref):
    scores = lax.dot_general(
        q_ref[...], k_ref[...], (((1,), (1,)), ((), ())), preferred_element_type=jnp.float32
    ) * (1.0 / math.sqrt(HD))
    raw = jnp.exp(scores - jnp.max(scores, axis=-1, keepdims=True))
    total = jnp.sum(raw, axis=-1, keepdims=True)
    mixed = jnp.dot(raw.astype(jnp.bfloat16), v_ref[...], preferred_element_type=jnp.float32)
    o_ref[...] = (mixed / total).astype(o_ref.dtype)


def attend_heads(packed, local_heads):
    frames = packed.shape[0]
    rows = 256
    return pl.pallas_call(
        attend_kernel,
        grid=(local_heads, frames // rows),
        in_specs=[
            pl.BlockSpec((rows, HD), lambda h, i: (i, h)),
            pl.BlockSpec((frames, HD), lambda h, i: (0, local_heads + h)),
            pl.BlockSpec((frames, HD), lambda h, i: (0, 2 * local_heads + h)),
        ],
        out_specs=pl.BlockSpec((rows, HD), lambda h, i: (i, h)),
        out_shape=jax.ShapeDtypeStruct((frames, local_heads * HD), jnp.bfloat16),
        cost_estimate=pl.CostEstimate(
            flops=4 * local_heads * frames * frames * HD,
            bytes_accessed=8 * frames * local_heads * HD,
            transcendentals=local_heads * frames * frames,
        ),
        name="attend_heads",
    )(packed, packed, packed)


def attention(queries, keys, values):
    n_ctx = lax.axis_size("ctx")
    tok_count, width = queries.shape
    local_heads = HEADS // n_ctx
    piece = width // n_ctx
    outgoing = jnp.concatenate(
        [jnp.transpose(a.reshape(tok_count, n_ctx, piece), (1, 0, 2)) for a in (queries, keys, values)],
        axis=-1,
    )
    arrived = lax.all_to_all(outgoing, "ctx", split_axis=0, concat_axis=0, tiled=True)
    mixed = attend_heads(arrived.reshape(n_ctx * tok_count, 3 * piece), local_heads)
    returned = lax.all_to_all(
        mixed.reshape(n_ctx, tok_count, piece), "ctx", split_axis=0, concat_axis=0, tiled=True
    )
    return jnp.transpose(returned, (1, 0, 2)).reshape(tok_count, width)


def swap_core(a):
    return lax.ppermute(a, "exp", [(i, i ^ 1) for i in range(4)])


def swap_x(a):
    return lax.ppermute(a, "exp", [(i, i ^ 2) for i in range(4)])


def swap_y(a):
    return lax.ppermute(a, "ctx", [(i, i ^ 1) for i in range(8)])


def turn_z(a, steps):
    return lax.ppermute(a, "ctx", [(i, (i + 2 * steps) % 8) for i in range(8)])


def ffn_kernel(*refs, n_parts):
    parts = refs[:n_parts]
    gate_ref, first_ref, second_ref, own_ref, other_ref, rows_ref, total_ref = refs[n_parts:]
    expert, block = pl.program_id(0), pl.program_id(1)
    first_step = (expert == 0) & (block == 0)
    last_step = (expert == pl.num_programs(0) - 1) & (block == pl.num_programs(1) - 1)

    @pl.when(first_step)
    def _():
        at = 0
        for part in parts:
            size = part.shape[0]
            rows_ref[at : at + size, :] = part[...]
            at += size

    inner = gelu_tanh(
        jnp.dot(rows_ref[...], first_ref[0], preferred_element_type=jnp.float32)
    ) * gate_ref[0]
    product = jnp.dot(
        inner.astype(jnp.bfloat16), second_ref[0], preferred_element_type=jnp.float32
    )

    @pl.when(first_step)
    def _():
        total_ref[...] = product

    @pl.when(jnp.logical_not(first_step))
    def _():
        total_ref[...] += product

    @pl.when(last_step)
    def _():
        half = own_ref.shape[0]
        own_ref[...] = total_ref[:half].astype(own_ref.dtype)
        other_ref[...] = total_ref[half:].astype(other_ref.dtype)


def dense_ffn(parts, gate, w_in, w_out):
    rows = sum(p.shape[0] for p in parts)
    n_exp, width, inner = w_in.shape
    cut = 512
    whole = lambda e, f: (0, 0)
    half = jax.ShapeDtypeStruct((rows // 2, width), jnp.bfloat16)
    return pl.pallas_call(
        functools.partial(ffn_kernel, n_parts=len(parts)),
        grid=(n_exp, inner // cut),
        in_specs=[pl.BlockSpec(p.shape, whole, pipeline_mode=pl.Buffered(1)) for p in parts]
        + [
            pl.BlockSpec((1, rows, 1), lambda e, f: (e, 0, 0)),
            pl.BlockSpec((1, width, cut), lambda e, f: (e, 0, f)),
            pl.BlockSpec((1, cut, width), lambda e, f: (e, f, 0)),
        ],
        out_specs=[pl.BlockSpec(half.shape, whole)] * 2,
        out_shape=[half, half],
        scratch_shapes=[
            pltpu.VMEM((rows, width), jnp.bfloat16),
            pltpu.VMEM((rows, width), jnp.float32),
        ],
        compiler_params=pltpu.CompilerParams(vmem_limit_bytes=56 << 20),
        cost_estimate=pl.CostEstimate(
            flops=4 * n_exp * rows * width * inner,
            bytes_accessed=4 * n_exp * width * inner + 4 * rows * width,
            transcendentals=n_exp * rows * inner,
        ),
        name="dense_ffn",
    )(*parts, gate, w_in, w_out)


def gather_plane(a):
    half = a.shape[0] // 2
    by_y, by_x = swap_y(a), swap_x(a)
    corner_x, corner_y = swap_x(by_y[:half]), swap_y(by_x[half:])
    mine = [a, by_y, by_x, corner_x, corner_y]
    return mine + [swap_core(p) for p in mine]


def reduce_plane(own_half, other_half, tok_count):
    half = tok_count // 2
    both = own_half.astype(jnp.float32) + swap_core(other_half).astype(jnp.float32)
    mine, to_y, to_x = (both[i * tok_count : (i + 1) * tok_count] for i in range(3))
    corner = both[3 * tok_count :].astype(jnp.bfloat16)
    from_x, from_y = swap_x(corner[:half]), swap_y(corner[half:])
    to_y = to_y.at[:half].add(from_x.astype(jnp.float32)).astype(jnp.bfloat16)
    to_x = to_x.at[half:].add(from_y.astype(jnp.float32)).astype(jnp.bfloat16)
    return mine + swap_y(to_y).astype(jnp.float32) + swap_x(to_x).astype(jnp.float32)


def dense_sum(hidden_f, normed, expert_ids, gate_weights, w_in, w_out):
    tok_count, _ = normed.shape
    n_local = w_in.shape[0]
    small = jnp.concatenate([expert_ids[0].astype(jnp.float32).T, gate_weights[0].T], axis=0)
    by_y = swap_y(small)
    small = jnp.stack([small, by_y])
    small = jnp.concatenate([small, swap_x(small)])
    small = jnp.concatenate([small, swap_core(small)])
    small = [small] + [turn_z(small, k) for k in range(1, 4)]
    local_ids = (
        lax.axis_index("exp") * n_local + jnp.arange(n_local, dtype=jnp.int32)
    ).astype(jnp.float32)

    gathered, ring = [], normed
    for k in range(4):
        if k:
            ring = turn_z(ring, 1)
        gathered.append(gather_plane(ring))
    total = hidden_f
    for k in range(4):
        ids = jnp.transpose(small[k][:, 0:2], (1, 0, 2)).reshape(2, -1)
        gates = jnp.transpose(small[k][:, 2:4], (1, 0, 2)).reshape(2, -1)
        gate = jnp.sum(
            jnp.where(ids[None] == local_ids[:, None, None], gates[None], 0.0), axis=1
        )
        own_half, other_half = dense_ffn(gathered[k], gate[..., None], w_in, w_out)
        plane = reduce_plane(own_half, other_half, tok_count)
        if k:
            plane = turn_z(plane.astype(jnp.bfloat16), -k).astype(jnp.float32)
        total = total + plane
    return total


def on_device(frames, queries, keys, values, expert_ids, gate_weights, w_in, w_out):
    attended = attention(queries[0], keys[0], values[0]).astype(jnp.float32)
    hidden_state = (frames[0].astype(jnp.float32) + attended).astype(jnp.bfloat16)
    hidden_f = hidden_state.astype(jnp.float32)
    normed = (
        hidden_f * lax.rsqrt(jnp.mean(hidden_f * hidden_f, axis=-1, keepdims=True) + EPSILON)
    ).astype(jnp.bfloat16)
    dense = lax.axis_size("ctx") == 8 and lax.axis_size("exp") == 4
    ffn = dense_sum if dense else routed_ffn
    layer_out = ffn(hidden_f, normed, expert_ids, gate_weights, w_in, w_out)
    return layer_out.astype(jnp.bfloat16)[None]


def solution(mesh):
    rows = P("exp", "ctx", None)
    in_specs = (rows,) * 6 + (P("exp", None, "ctx"), P("exp", "ctx", None))
    return jax.shard_map(
        on_device, mesh=mesh, in_specs=in_specs, out_specs=rows, check_vma=False
    )
```

```python
import functools
import math

import jax
import jax.numpy as jnp
from jax import lax
from jax.experimental import pallas as pl
from jax.experimental.pallas import tpu as pltpu
from jax.sharding import PartitionSpec as P

HEADS = 16
HD = 128


EPSILON = 1e-05


def gelu_tanh(values_in):
    return jax.nn.gelu(values_in, approximate=True)


def expert_partial(gathered, live_flags, first_w, second_w):
    total_rows = gathered.shape[0]
    out_width = second_w.shape[1]
    padded_rows = -(-total_rows // 128) * 128
    position = jnp.cumsum(live_flags) - 1
    live_count = jnp.sum(live_flags)
    target = jnp.where(live_flags > 0, position, padded_rows)
    order_idx = (
        jnp.zeros((padded_rows,), jnp.int32)
        .at[target]
        .set(jnp.arange(total_rows, dtype=jnp.int32), mode="drop")
    )
    block_count = (live_count + 127) // 128

    def one_block(block_num, packed):
        picked = lax.dynamic_slice_in_dim(order_idx, block_num * 128, 128)
        inputs = jnp.take(gathered, picked, axis=0)
        inner_act = gelu_tanh(jnp.dot(inputs, first_w, preferred_element_type=jnp.float32)).astype(
            jnp.bfloat16
        )
        output = jnp.dot(inner_act, second_w, preferred_element_type=jnp.float32).astype(
            jnp.bfloat16
        )
        return lax.dynamic_update_slice_in_dim(packed, output, block_num * 128, 0)

    packed = lax.fori_loop(
        0, block_count, one_block, jnp.zeros((padded_rows, out_width), jnp.bfloat16)
    )
    back_idx = jnp.where(live_flags > 0, position, 0).astype(jnp.int32)
    unpacked = jnp.take(packed, back_idx, axis=0)
    return jnp.where((live_flags > 0)[:, None], unpacked, jnp.zeros_like(unpacked))


def routed_ffn(hidden_f, normed, expert_ids, gate_weights, w_in, w_out):
    tok_count, model_width = normed.shape
    slot_ids = expert_ids[0].reshape(-1)
    slot_count = slot_ids.shape[0]
    exp_local = w_in.shape[0]
    num_experts = exp_local * lax.axis_size("exp")
    capacity = 2 * (slot_count // num_experts)
    onehot = (slot_ids[:, None] == jnp.arange(num_experts, dtype=jnp.int32)[None, :]).astype(
        jnp.int32
    )
    slot_rank = jnp.sum((jnp.cumsum(onehot, axis=0) - onehot) * onehot, axis=1)
    target = slot_ids * capacity + slot_rank
    send_matrix = (
        jnp.arange(num_experts * capacity, dtype=jnp.int32)[:, None] == target[None, :]
    ).astype(jnp.int32)
    token_matrix = send_matrix.reshape(num_experts * capacity, tok_count, 2).sum(-1)
    outgoing = jnp.dot(
        token_matrix.astype(jnp.bfloat16), normed, preferred_element_type=jnp.float32
    ).astype(jnp.bfloat16)
    outgoing = outgoing.reshape(num_experts, capacity, model_width)
    occupied = jnp.sum(send_matrix, axis=1).reshape(num_experts, capacity)
    arrived, arrived_flags = (
        lax.all_to_all(outgoing, "exp", split_axis=0, concat_axis=1, tiled=True),
        lax.all_to_all(occupied, "exp", split_axis=0, concat_axis=1, tiled=True),
    )
    gathered, gathered_flags = (
        lax.all_gather(arrived, "ctx", axis=1, tiled=True),
        lax.all_gather(arrived_flags, "ctx", axis=1, tiled=True),
    )
    summed_list = []
    for local_num in range(exp_local):
        partial_value = expert_partial(
            gathered[local_num], gathered_flags[local_num], w_in[local_num], w_out[local_num]
        )
        summed_list.append(
            lax.psum_scatter(partial_value, "ctx", scatter_dimension=0, tiled=True)
            .astype(jnp.float32)
            .astype(jnp.bfloat16)
        )
    summed = jnp.stack(summed_list)
    returned = lax.all_to_all(summed, "exp", split_axis=1, concat_axis=0, tiled=True)
    slot_out = jnp.dot(
        send_matrix.T.astype(jnp.bfloat16),
        returned.reshape(num_experts * capacity, model_width),
        preferred_element_type=jnp.float32,
    )
    tok_out = slot_out.reshape(tok_count, 2, model_width)
    gates = gate_weights[0]
    return hidden_f + gates[:, 0:1] * tok_out[:, 0] + gates[:, 1:2] * tok_out[:, 1]


def attend_kernel(q_ref, k_ref, v_ref, o_ref):
    scores = lax.dot_general(
        q_ref[...], k_ref[...], (((1,), (1,)), ((), ())), preferred_element_type=jnp.float32
    ) * (1.0 / math.sqrt(HD))
    raw = jnp.exp(scores - jnp.max(scores, axis=-1, keepdims=True))
    total = jnp.sum(raw, axis=-1, keepdims=True)
    mixed = jnp.dot(raw.astype(jnp.bfloat16), v_ref[...], preferred_element_type=jnp.float32)
    o_ref[...] = (mixed / total).astype(o_ref.dtype)


def attend_heads(packed, local_heads):
    frames = packed.shape[0]
    rows = 256
    return pl.pallas_call(
        attend_kernel,
        grid=(local_heads, frames // rows),
        in_specs=[
            pl.BlockSpec((rows, HD), lambda h, i: (i, h)),
            pl.BlockSpec((frames, HD), lambda h, i: (0, local_heads + h)),
            pl.BlockSpec((frames, HD), lambda h, i: (0, 2 * local_heads + h)),
        ],
        out_specs=pl.BlockSpec((rows, HD), lambda h, i: (i, h)),
        out_shape=jax.ShapeDtypeStruct((frames, local_heads * HD), jnp.bfloat16),
        cost_estimate=pl.CostEstimate(
            flops=4 * local_heads * frames * frames * HD,
            bytes_accessed=8 * frames * local_heads * HD,
            transcendentals=local_heads * frames * frames,
        ),
        name="attend_heads",
    )(packed, packed, packed)


def attention(queries, keys, values):
    n_ctx = lax.axis_size("ctx")
    tok_count, width = queries.shape
    local_heads = HEADS // n_ctx
    piece = width // n_ctx
    outgoing = jnp.concatenate(
        [jnp.transpose(a.reshape(tok_count, n_ctx, piece), (1, 0, 2)) for a in (queries, keys, values)],
        axis=-1,
    )
    arrived = lax.all_to_all(outgoing, "ctx", split_axis=0, concat_axis=0, tiled=True)
    mixed = attend_heads(arrived.reshape(n_ctx * tok_count, 3 * piece), local_heads)
    returned = lax.all_to_all(
        mixed.reshape(n_ctx, tok_count, piece), "ctx", split_axis=0, concat_axis=0, tiled=True
    )
    return jnp.transpose(returned, (1, 0, 2)).reshape(tok_count, width)


def swap_core(a):
    return lax.ppermute(a, "exp", [(i, i ^ 1) for i in range(4)])


def swap_x(a):
    return lax.ppermute(a, "exp", [(i, i ^ 2) for i in range(4)])


def swap_y(a):
    return lax.ppermute(a, "ctx", [(i, i ^ 1) for i in range(8)])


def turn_z(a, steps):
    return lax.ppermute(a, "ctx", [(i, (i + 2 * steps) % 8) for i in range(8)])


def gated_ffn(rows, gate, w_in, w_out):
    n_exp, inner, width = w_out.shape
    acts = [
        (
            gelu_tanh(jnp.dot(rows, w_in[e], preferred_element_type=jnp.float32))
            * gate[e][:, None]
        ).astype(jnp.bfloat16)
        for e in range(n_exp)
    ]
    return jnp.dot(
        jnp.concatenate(acts, axis=1),
        w_out.reshape(n_exp * inner, width),
        preferred_element_type=jnp.float32,
    ).astype(jnp.bfloat16)


def after(gate_value, values):
    return lax.optimization_barrier((gate_value, values))


def dense_sum(hidden_f, normed, expert_ids, gate_weights, w_in, w_out):
    tok_count, _ = normed.shape
    half = tok_count // 2
    n_local = w_in.shape[0]
    f32, bf16 = jnp.float32, jnp.bfloat16
    small = jnp.concatenate([expert_ids[0].astype(f32).T, gate_weights[0].T], axis=0)
    small = jnp.stack([small, swap_y(small)])
    small = jnp.concatenate([small, swap_x(small)])
    small = jnp.stack([small, swap_core(small)])
    small = [small] + [turn_z(small, k) for k in range(1, 4)]
    local_ids = (
        lax.axis_index("exp") * n_local + jnp.arange(n_local, dtype=jnp.int32)
    ).astype(f32)

    def gate_of(slot, core):
        picked = small[slot][core]
        ids = jnp.transpose(picked[:, 0:2], (1, 0, 2)).reshape(2, -1)
        gates = jnp.transpose(picked[:, 2:4], (1, 0, 2)).reshape(2, -1)
        return jnp.sum(
            jnp.where(ids[None] == local_ids[:, None, None], gates[None], 0.0), axis=1
        )

    def neighbours(rows):
        return [rows, swap_y(rows), swap_x(rows)]

    def corners(near):
        return [swap_x(near[1][:half]), swap_y(near[2][half:])]

    ring = [normed, turn_z(normed, 1), None, None]
    near, corner, own, other = [None] * 4, [None] * 4, [None] * 4, [None] * 4
    near[0] = neighbours(normed)
    corner[0] = corners(near[0])
    own[0] = jnp.concatenate(near[0] + corner[0])
    other[0] = swap_core(own[0])
    near[1] = neighbours(ring[1])
    ring[2] = turn_z(ring[1], 1)

    out_own, crossed, parts, flows, planes = [None] * 4, [None] * 4, [None] * 4, [None] * 4, [None] * 4

    def split(slot):
        both = out_own[slot].astype(f32) + crossed[slot].astype(f32)
        mine, to_y, to_x = (both[i * tok_count : (i + 1) * tok_count] for i in range(3))
        last = both[3 * tok_count :].astype(bf16)
        return mine, to_y, to_x, [swap_x(last[:half]), swap_y(last[half:])]

    def pass_on(slot):
        mine, to_y, to_x, (from_x, from_y) = parts[slot]
        to_y = to_y.at[:half].add(from_x.astype(f32)).astype(bf16)
        to_x = to_x.at[half:].add(from_y.astype(f32)).astype(bf16)
        return mine, swap_y(to_y), swap_x(to_x)

    def finish(slot):
        mine, from_y, from_x = flows[slot]
        plane = mine + from_y.astype(f32) + from_x.astype(f32)
        return turn_z(plane.astype(bf16), -slot) if slot else plane

    for tick in range(8):
        slot, core = divmod(tick, 2)
        rows = other[slot] if core else own[slot]
        out = gated_ffn(rows, gate_of(slot, core), w_in, w_out)
        step = tick + 1
        state = dict(near=near, corner=corner, ring=ring, crossed=crossed, parts=parts, flows=flows)
        wanted = []
        if step % 2 and step <= 5:
            wanted.append(("near", (step + 1) // 2))
        if step % 2 == 0 and step <= 6:
            wanted += [("corner", step // 2), ("near", step // 2)]
            if step <= 4:
                wanted.append(("ring", (step + 2) // 2))
        if step % 2 and step >= 3:
            wanted.append(("crossed", (step - 3) // 2))
        if step % 2 == 0 and step >= 4:
            wanted.append(("parts", (step - 4) // 2))
        if step % 2 and step >= 5:
            wanted.append(("flows", (step - 5) // 2))
        out, values = after(out, [state[name][at] for name, at in wanted])
        for (name, at), value in zip(wanted, values):
            state[name][at] = value
        if core:
            crossed[slot] = swap_core(out)
        else:
            out_own[slot] = out
        if step % 2 and step <= 5:
            corner[(step + 1) // 2] = corners(near[(step + 1) // 2])
        if step % 2 == 0 and step <= 6:
            at = step // 2
            own[at] = jnp.concatenate(near[at] + corner[at])
            other[at] = swap_core(own[at])
            if at < 3:
                near[at + 1] = neighbours(ring[at + 1])
                if at < 2:
                    ring[at + 2] = turn_z(ring[at + 1], 1)
        if step % 2 and step >= 3:
            parts[(step - 3) // 2] = split((step - 3) // 2)
        if step % 2 == 0 and step >= 4:
            flows[(step - 4) // 2] = pass_on((step - 4) // 2)
        if step % 2 and step >= 5:
            planes[(step - 5) // 2] = finish((step - 5) // 2)
    parts[3] = split(3)
    planes[1] = finish(1) if planes[1] is None else planes[1]
    for slot in (2, 3):
        if flows[slot] is None:
            flows[slot] = pass_on(slot)
        planes[slot] = finish(slot)
    total = hidden_f
    for plane in planes:
        total = total + plane.astype(f32)
    return total


def on_device(frames, queries, keys, values, expert_ids, gate_weights, w_in, w_out):
    attended = attention(queries[0], keys[0], values[0]).astype(jnp.float32)
    hidden_state = (frames[0].astype(jnp.float32) + attended).astype(jnp.bfloat16)
    hidden_f = hidden_state.astype(jnp.float32)
    normed = (
        hidden_f * lax.rsqrt(jnp.mean(hidden_f * hidden_f, axis=-1, keepdims=True) + EPSILON)
    ).astype(jnp.bfloat16)
    dense = lax.axis_size("ctx") == 8 and lax.axis_size("exp") == 4
    ffn = dense_sum if dense else routed_ffn
    layer_out = ffn(hidden_f, normed, expert_ids, gate_weights, w_in, w_out)
    return layer_out.astype(jnp.bfloat16)[None]


def solution(mesh):
    rows = P("exp", "ctx", None)
    in_specs = (rows,) * 6 + (P("exp", None, "ctx"), P("exp", "ctx", None))
    return jax.shard_map(
        on_device, mesh=mesh, in_specs=in_specs, out_specs=rows, check_vma=False
    )
```

```python
import functools
import math

import jax
import jax.numpy as jnp
from jax import lax
from jax.experimental import pallas as pl
from jax.experimental.pallas import tpu as pltpu
from jax.sharding import PartitionSpec as P

HEADS = 16
HD = 128


EPSILON = 1e-05


def gelu_tanh(values_in):
    return jax.nn.gelu(values_in, approximate=True)


def expert_partial(gathered, live_flags, first_w, second_w):
    total_rows = gathered.shape[0]
    out_width = second_w.shape[1]
    padded_rows = -(-total_rows // 128) * 128
    position = jnp.cumsum(live_flags) - 1
    live_count = jnp.sum(live_flags)
    target = jnp.where(live_flags > 0, position, padded_rows)
    order_idx = (
        jnp.zeros((padded_rows,), jnp.int32)
        .at[target]
        .set(jnp.arange(total_rows, dtype=jnp.int32), mode="drop")
    )
    block_count = (live_count + 127) // 128

    def one_block(block_num, packed):
        picked = lax.dynamic_slice_in_dim(order_idx, block_num * 128, 128)
        inputs = jnp.take(gathered, picked, axis=0)
        inner_act = gelu_tanh(jnp.dot(inputs, first_w, preferred_element_type=jnp.float32)).astype(
            jnp.bfloat16
        )
        output = jnp.dot(inner_act, second_w, preferred_element_type=jnp.float32).astype(
            jnp.bfloat16
        )
        return lax.dynamic_update_slice_in_dim(packed, output, block_num * 128, 0)

    packed = lax.fori_loop(
        0, block_count, one_block, jnp.zeros((padded_rows, out_width), jnp.bfloat16)
    )
    back_idx = jnp.where(live_flags > 0, position, 0).astype(jnp.int32)
    unpacked = jnp.take(packed, back_idx, axis=0)
    return jnp.where((live_flags > 0)[:, None], unpacked, jnp.zeros_like(unpacked))


def routed_ffn(hidden_f, normed, expert_ids, gate_weights, w_in, w_out):
    tok_count, model_width = normed.shape
    slot_ids = expert_ids[0].reshape(-1)
    slot_count = slot_ids.shape[0]
    exp_local = w_in.shape[0]
    num_experts = exp_local * lax.axis_size("exp")
    capacity = 2 * (slot_count // num_experts)
    onehot = (slot_ids[:, None] == jnp.arange(num_experts, dtype=jnp.int32)[None, :]).astype(
        jnp.int32
    )
    slot_rank = jnp.sum((jnp.cumsum(onehot, axis=0) - onehot) * onehot, axis=1)
    target = slot_ids * capacity + slot_rank
    send_matrix = (
        jnp.arange(num_experts * capacity, dtype=jnp.int32)[:, None] == target[None, :]
    ).astype(jnp.int32)
    token_matrix = send_matrix.reshape(num_experts * capacity, tok_count, 2).sum(-1)
    outgoing = jnp.dot(
        token_matrix.astype(jnp.bfloat16), normed, preferred_element_type=jnp.float32
    ).astype(jnp.bfloat16)
    outgoing = outgoing.reshape(num_experts, capacity, model_width)
    occupied = jnp.sum(send_matrix, axis=1).reshape(num_experts, capacity)
    arrived, arrived_flags = (
        lax.all_to_all(outgoing, "exp", split_axis=0, concat_axis=1, tiled=True),
        lax.all_to_all(occupied, "exp", split_axis=0, concat_axis=1, tiled=True),
    )
    gathered, gathered_flags = (
        lax.all_gather(arrived, "ctx", axis=1, tiled=True),
        lax.all_gather(arrived_flags, "ctx", axis=1, tiled=True),
    )
    summed_list = []
    for local_num in range(exp_local):
        partial_value = expert_partial(
            gathered[local_num], gathered_flags[local_num], w_in[local_num], w_out[local_num]
        )
        summed_list.append(
            lax.psum_scatter(partial_value, "ctx", scatter_dimension=0, tiled=True)
            .astype(jnp.float32)
            .astype(jnp.bfloat16)
        )
    summed = jnp.stack(summed_list)
    returned = lax.all_to_all(summed, "exp", split_axis=1, concat_axis=0, tiled=True)
    slot_out = jnp.dot(
        send_matrix.T.astype(jnp.bfloat16),
        returned.reshape(num_experts * capacity, model_width),
        preferred_element_type=jnp.float32,
    )
    tok_out = slot_out.reshape(tok_count, 2, model_width)
    gates = gate_weights[0]
    return hidden_f + gates[:, 0:1] * tok_out[:, 0] + gates[:, 1:2] * tok_out[:, 1]


def attend_kernel(q_ref, k_ref, v_ref, o_ref):
    scores = lax.dot_general(
        q_ref[...], k_ref[...], (((1,), (1,)), ((), ())), preferred_element_type=jnp.float32
    ) * (1.0 / math.sqrt(HD))
    raw = jnp.exp(scores - jnp.max(scores, axis=-1, keepdims=True))
    total = jnp.sum(raw, axis=-1, keepdims=True)
    mixed = jnp.dot(raw.astype(jnp.bfloat16), v_ref[...], preferred_element_type=jnp.float32)
    o_ref[...] = (mixed / total).astype(o_ref.dtype)


def attend_heads(packed, local_heads):
    frames = packed.shape[0]
    rows = 256
    return pl.pallas_call(
        attend_kernel,
        grid=(local_heads, frames // rows),
        in_specs=[
            pl.BlockSpec((rows, HD), lambda h, i: (i, h)),
            pl.BlockSpec((frames, HD), lambda h, i: (0, local_heads + h)),
            pl.BlockSpec((frames, HD), lambda h, i: (0, 2 * local_heads + h)),
        ],
        out_specs=pl.BlockSpec((rows, HD), lambda h, i: (i, h)),
        out_shape=jax.ShapeDtypeStruct((frames, local_heads * HD), jnp.bfloat16),
        cost_estimate=pl.CostEstimate(
            flops=4 * local_heads * frames * frames * HD,
            bytes_accessed=8 * frames * local_heads * HD,
            transcendentals=local_heads * frames * frames,
        ),
        name="attend_heads",
    )(packed, packed, packed)


def attention(queries, keys, values):
    n_ctx = lax.axis_size("ctx")
    tok_count, width = queries.shape
    local_heads = HEADS // n_ctx
    piece = width // n_ctx
    outgoing = jnp.concatenate(
        [jnp.transpose(a.reshape(tok_count, n_ctx, piece), (1, 0, 2)) for a in (queries, keys, values)],
        axis=-1,
    )
    arrived = lax.all_to_all(outgoing, "ctx", split_axis=0, concat_axis=0, tiled=True)
    mixed = attend_heads(arrived.reshape(n_ctx * tok_count, 3 * piece), local_heads)
    returned = lax.all_to_all(
        mixed.reshape(n_ctx, tok_count, piece), "ctx", split_axis=0, concat_axis=0, tiled=True
    )
    return jnp.transpose(returned, (1, 0, 2)).reshape(tok_count, width)


def swap_core(a):
    return lax.ppermute(a, "exp", [(i, i ^ 1) for i in range(4)])


def swap_x(a):
    return lax.ppermute(a, "exp", [(i, i ^ 2) for i in range(4)])


def swap_y(a):
    return lax.ppermute(a, "ctx", [(i, i ^ 1) for i in range(8)])


def turn_z(a, steps):
    return lax.ppermute(a, "ctx", [(i, (i + 2 * steps) % 8) for i in range(8)])


def gated_ffn(rows, gate, w_in, w_out):
    n_exp, inner, width = w_out.shape
    acts = [
        (
            gelu_tanh(jnp.dot(rows, w_in[e], preferred_element_type=jnp.float32))
            * gate[e][:, None]
        ).astype(jnp.bfloat16)
        for e in range(n_exp)
    ]
    return jnp.dot(
        jnp.concatenate(acts, axis=1),
        w_out.reshape(n_exp * inner, width),
        preferred_element_type=jnp.float32,
    ).astype(jnp.bfloat16)


def dense_sum(hidden_f, normed, expert_ids, gate_weights, w_in, w_out):
    tok_count, _ = normed.shape
    half = tok_count // 2
    n_local = w_in.shape[0]
    f32, bf16 = jnp.float32, jnp.bfloat16
    small = jnp.concatenate([expert_ids[0].astype(f32).T, gate_weights[0].T], axis=0)
    small = jnp.stack([small, swap_y(small)])
    small = jnp.concatenate([small, swap_x(small)])
    small = jnp.stack([small, swap_core(small)])
    small = [small] + [turn_z(small, k) for k in range(1, 4)]
    local_ids = (
        lax.axis_index("exp") * n_local + jnp.arange(n_local, dtype=jnp.int32)
    ).astype(f32)

    def gate_of(slot, core):
        picked = small[slot][core]
        ids = jnp.transpose(picked[:, 0:2], (1, 0, 2)).reshape(2, -1)
        gates = jnp.transpose(picked[:, 2:4], (1, 0, 2)).reshape(2, -1)
        return jnp.sum(
            jnp.where(ids[None] == local_ids[:, None, None], gates[None], 0.0), axis=1
        )

    def neighbours(rows):
        return [rows, swap_y(rows), swap_x(rows)]

    def corners(near):
        return [swap_x(near[1][:half]), swap_y(near[2][half:])]

    def rows_of(near, corner):
        return jnp.concatenate(near + corner)

    def split(own_out, crossed):
        both = own_out.astype(f32) + crossed.astype(f32)
        mine, to_y, to_x = (both[i * tok_count : (i + 1) * tok_count] for i in range(3))
        last = both[3 * tok_count :].astype(bf16)
        return mine, to_y, to_x, swap_x(last[:half]), swap_y(last[half:])

    def pass_on(parts):
        mine, to_y, to_x, from_x, from_y = parts
        to_y = to_y.at[:half].add(from_x.astype(f32)).astype(bf16)
        to_x = to_x.at[half:].add(from_y.astype(f32)).astype(bf16)
        return mine, swap_y(to_y), swap_x(to_x)

    def finish(slot, flow):
        mine, from_y, from_x = flow
        plane = mine + from_y.astype(f32) + from_x.astype(f32)
        return turn_z(plane.astype(bf16), -slot) if slot else plane

    state = {"ring1": turn_z(normed, 1), "near0": neighbours(normed)}

    def act(name, slot, *operands):
        key = f"{name}{slot}"
        if name == "ring":
            state[key] = turn_z(*operands, 1)
        elif name == "near":
            state[key] = neighbours(*operands)
        elif name == "corner":
            state[key] = corners(*operands)
        elif name == "own":
            state[key] = rows_of(*operands)
            state[f"other{slot}"] = swap_core(state[key])
        elif name == "cross":
            state[key] = swap_core(*operands)
        elif name == "parts":
            state[key] = split(*operands)
        elif name == "flow":
            state[key] = pass_on(*operands)
        elif name == "plane":
            state[key] = finish(slot, *operands)

    needs = {
        "ring": lambda k: [f"ring{k - 1}"],
        "near": lambda k: [f"ring{k}"],
        "corner": lambda k: [f"near{k}"],
        "own": lambda k: [f"near{k}", f"corner{k}"],
        "cross": lambda k: [f"other_out{k}"],
        "parts": lambda k: [f"own_out{k}", f"cross{k}"],
        "flow": lambda k: [f"parts{k}"],
        "plane": lambda k: [f"flow{k}"],
    }
    steps = [
        None, None, ("own", 0), None,
        ("own", 1), ("other", 1), ("own", 2), ("other", 2),
        ("own", 3), ("other", 3), ("other", 0),
        None, None, None, None,
    ]
    events = [
        [],
        [("corner", 0), ("near", 1), ("ring", 2)],
        [("own", 0)],
        [("corner", 1), ("near", 2), ("ring", 3)],
        [("own", 1)],
        [("corner", 2), ("near", 3)],
        [("own", 2), ("cross", 1)],
        [("parts", 1), ("corner", 3)],
        [("own", 3), ("cross", 2), ("flow", 1)],
        [("parts", 2), ("plane", 1)],
        [("cross", 3), ("flow", 2)],
        [("parts", 3), ("cross", 0), ("plane", 2)],
        [("flow", 3), ("parts", 0)],
        [("plane", 3), ("flow", 0)],
        [("plane", 0)],
    ]
    due = {1: ["ring1"], 11: ["plane1"], 14: ["plane2"]}
    for number, step in enumerate(steps):
        if number:
            keys = {key for name, slot in events[number] for key in needs[name](slot)}
            keys |= set(due.get(number, []))
            if steps[number - 1]:
                keys.add("{}_out{}".format(*steps[number - 1]))
            if step:
                keys.add("{}{}".format(*step))
            keys = sorted(keys & set(state))
            state.update(zip(keys, lax.optimization_barrier([state[key] for key in keys])))
        for name, slot in events[number]:
            act(name, slot, *(state[key] for key in needs[name](slot)))
        if step:
            which, k = step
            state[f"{which}_out{k}"] = gated_ffn(
                state[f"{which}{k}"], gate_of(k, int(which == "other")), w_in, w_out
            )
    total = hidden_f
    for k in range(4):
        total = total + state[f"plane{k}"].astype(f32)
    return total


def on_device(frames, queries, keys, values, expert_ids, gate_weights, w_in, w_out):
    attended = attention(queries[0], keys[0], values[0]).astype(jnp.float32)
    hidden_state = (frames[0].astype(jnp.float32) + attended).astype(jnp.bfloat16)
    hidden_f = hidden_state.astype(jnp.float32)
    normed = (
        hidden_f * lax.rsqrt(jnp.mean(hidden_f * hidden_f, axis=-1, keepdims=True) + EPSILON)
    ).astype(jnp.bfloat16)
    dense = lax.axis_size("ctx") == 8 and lax.axis_size("exp") == 4
    ffn = dense_sum if dense else routed_ffn
    layer_out = ffn(hidden_f, normed, expert_ids, gate_weights, w_in, w_out)
    return layer_out.astype(jnp.bfloat16)[None]


def solution(mesh):
    rows = P("exp", "ctx", None)
    in_specs = (rows,) * 6 + (P("exp", None, "ctx"), P("exp", "ctx", None))
    return jax.shard_map(
        on_device, mesh=mesh, in_specs=in_specs, out_specs=rows, check_vma=False
    )
```

```python
import functools
import math

import jax
import jax.numpy as jnp
from jax import lax
from jax.experimental import pallas as pl
from jax.experimental.pallas import tpu as pltpu
from jax.sharding import PartitionSpec as P

HEADS = 16
HD = 128


EPSILON = 1e-05


def gelu_tanh(values_in):
    return jax.nn.gelu(values_in, approximate=True)


def expert_partial(gathered, live_flags, first_w, second_w):
    total_rows = gathered.shape[0]
    out_width = second_w.shape[1]
    padded_rows = -(-total_rows // 128) * 128
    position = jnp.cumsum(live_flags) - 1
    live_count = jnp.sum(live_flags)
    target = jnp.where(live_flags > 0, position, padded_rows)
    order_idx = (
        jnp.zeros((padded_rows,), jnp.int32)
        .at[target]
        .set(jnp.arange(total_rows, dtype=jnp.int32), mode="drop")
    )
    block_count = (live_count + 127) // 128

    def one_block(block_num, packed):
        picked = lax.dynamic_slice_in_dim(order_idx, block_num * 128, 128)
        inputs = jnp.take(gathered, picked, axis=0)
        inner_act = gelu_tanh(jnp.dot(inputs, first_w, preferred_element_type=jnp.float32)).astype(
            jnp.bfloat16
        )
        output = jnp.dot(inner_act, second_w, preferred_element_type=jnp.float32).astype(
            jnp.bfloat16
        )
        return lax.dynamic_update_slice_in_dim(packed, output, block_num * 128, 0)

    packed = lax.fori_loop(
        0, block_count, one_block, jnp.zeros((padded_rows, out_width), jnp.bfloat16)
    )
    back_idx = jnp.where(live_flags > 0, position, 0).astype(jnp.int32)
    unpacked = jnp.take(packed, back_idx, axis=0)
    return jnp.where((live_flags > 0)[:, None], unpacked, jnp.zeros_like(unpacked))


def routed_ffn(hidden_f, normed, expert_ids, gate_weights, w_in, w_out):
    tok_count, model_width = normed.shape
    slot_ids = expert_ids[0].reshape(-1)
    slot_count = slot_ids.shape[0]
    exp_local = w_in.shape[0]
    num_experts = exp_local * lax.axis_size("exp")
    capacity = 2 * (slot_count // num_experts)
    onehot = (slot_ids[:, None] == jnp.arange(num_experts, dtype=jnp.int32)[None, :]).astype(
        jnp.int32
    )
    slot_rank = jnp.sum((jnp.cumsum(onehot, axis=0) - onehot) * onehot, axis=1)
    target = slot_ids * capacity + slot_rank
    send_matrix = (
        jnp.arange(num_experts * capacity, dtype=jnp.int32)[:, None] == target[None, :]
    ).astype(jnp.int32)
    token_matrix = send_matrix.reshape(num_experts * capacity, tok_count, 2).sum(-1)
    outgoing = jnp.dot(
        token_matrix.astype(jnp.bfloat16), normed, preferred_element_type=jnp.float32
    ).astype(jnp.bfloat16)
    outgoing = outgoing.reshape(num_experts, capacity, model_width)
    occupied = jnp.sum(send_matrix, axis=1).reshape(num_experts, capacity)
    arrived, arrived_flags = (
        lax.all_to_all(outgoing, "exp", split_axis=0, concat_axis=1, tiled=True),
        lax.all_to_all(occupied, "exp", split_axis=0, concat_axis=1, tiled=True),
    )
    gathered, gathered_flags = (
        lax.all_gather(arrived, "ctx", axis=1, tiled=True),
        lax.all_gather(arrived_flags, "ctx", axis=1, tiled=True),
    )
    summed_list = []
    for local_num in range(exp_local):
        partial_value = expert_partial(
            gathered[local_num], gathered_flags[local_num], w_in[local_num], w_out[local_num]
        )
        summed_list.append(
            lax.psum_scatter(partial_value, "ctx", scatter_dimension=0, tiled=True)
            .astype(jnp.float32)
            .astype(jnp.bfloat16)
        )
    summed = jnp.stack(summed_list)
    returned = lax.all_to_all(summed, "exp", split_axis=1, concat_axis=0, tiled=True)
    slot_out = jnp.dot(
        send_matrix.T.astype(jnp.bfloat16),
        returned.reshape(num_experts * capacity, model_width),
        preferred_element_type=jnp.float32,
    )
    tok_out = slot_out.reshape(tok_count, 2, model_width)
    gates = gate_weights[0]
    return hidden_f + gates[:, 0:1] * tok_out[:, 0] + gates[:, 1:2] * tok_out[:, 1]


def attend_kernel(q_ref, k_ref, v_ref, o_ref):
    scores = lax.dot_general(
        q_ref[...], k_ref[...], (((1,), (1,)), ((), ())), preferred_element_type=jnp.float32
    ) * (1.0 / math.sqrt(HD))
    raw = jnp.exp(scores - jnp.max(scores, axis=-1, keepdims=True))
    total = jnp.sum(raw, axis=-1, keepdims=True)
    mixed = jnp.dot(raw.astype(jnp.bfloat16), v_ref[...], preferred_element_type=jnp.float32)
    o_ref[...] = (mixed / total).astype(o_ref.dtype)


def attend_heads(packed, local_heads):
    frames = packed.shape[0]
    rows = 256
    return pl.pallas_call(
        attend_kernel,
        grid=(local_heads, frames // rows),
        in_specs=[
            pl.BlockSpec((rows, HD), lambda h, i: (i, h)),
            pl.BlockSpec((frames, HD), lambda h, i: (0, local_heads + h)),
            pl.BlockSpec((frames, HD), lambda h, i: (0, 2 * local_heads + h)),
        ],
        out_specs=pl.BlockSpec((rows, HD), lambda h, i: (i, h)),
        out_shape=jax.ShapeDtypeStruct((frames, local_heads * HD), jnp.bfloat16),
        cost_estimate=pl.CostEstimate(
            flops=4 * local_heads * frames * frames * HD,
            bytes_accessed=8 * frames * local_heads * HD,
            transcendentals=local_heads * frames * frames,
        ),
        name="attend_heads",
    )(packed, packed, packed)


def attention(queries, keys, values):
    n_ctx = lax.axis_size("ctx")
    tok_count, width = queries.shape
    local_heads = HEADS // n_ctx
    piece = width // n_ctx
    outgoing = jnp.concatenate(
        [jnp.transpose(a.reshape(tok_count, n_ctx, piece), (1, 0, 2)) for a in (queries, keys, values)],
        axis=-1,
    )
    arrived = lax.all_to_all(outgoing, "ctx", split_axis=0, concat_axis=0, tiled=True)
    mixed = attend_heads(arrived.reshape(n_ctx * tok_count, 3 * piece), local_heads)
    returned = lax.all_to_all(
        mixed.reshape(n_ctx, tok_count, piece), "ctx", split_axis=0, concat_axis=0, tiled=True
    )
    return jnp.transpose(returned, (1, 0, 2)).reshape(tok_count, width)


def swap_core(a):
    return lax.ppermute(a, "exp", [(i, i ^ 1) for i in range(4)])


def swap_x(a):
    return lax.ppermute(a, "exp", [(i, i ^ 2) for i in range(4)])


def swap_y(a):
    return lax.ppermute(a, "ctx", [(i, i ^ 1) for i in range(8)])


def turn_z(a, steps):
    return lax.ppermute(a, "ctx", [(i, (i + 2 * steps) % 8) for i in range(8)])


def gated_ffn(rows, gate, w_in, w_out):
    n_exp, inner, width = w_out.shape
    acts = [
        (
            gelu_tanh(jnp.dot(rows, w_in[e], preferred_element_type=jnp.float32))
            * gate[e][:, None]
        ).astype(jnp.bfloat16)
        for e in range(n_exp)
    ]
    return jnp.dot(
        jnp.concatenate(acts, axis=1),
        w_out.reshape(n_exp * inner, width),
        preferred_element_type=jnp.float32,
    ).astype(jnp.bfloat16)


def dense_sum(hidden_f, normed, expert_ids, gate_weights, w_in, w_out):
    tok_count, _ = normed.shape
    half = tok_count // 2
    n_local = w_in.shape[0]
    f32, bf16 = jnp.float32, jnp.bfloat16
    small = jnp.concatenate([expert_ids[0].astype(f32).T, gate_weights[0].T], axis=0)
    small = jnp.stack([small, swap_y(small)])
    small = jnp.concatenate([small, swap_x(small)])
    small = jnp.stack([small, swap_core(small)])
    small = [small] + [turn_z(small, k) for k in range(1, 4)]
    local_ids = (
        lax.axis_index("exp") * n_local + jnp.arange(n_local, dtype=jnp.int32)
    ).astype(f32)

    def gate_of(slot, core):
        picked = small[slot][core]
        ids = jnp.transpose(picked[:, 0:2], (1, 0, 2)).reshape(2, -1)
        gates = jnp.transpose(picked[:, 2:4], (1, 0, 2)).reshape(2, -1)
        return jnp.sum(
            jnp.where(ids[None] == local_ids[:, None, None], gates[None], 0.0), axis=1
        )

    def neighbours(rows):
        return [rows, swap_y(rows), swap_x(rows)]

    def corners(near):
        return [swap_x(near[1][:half]), swap_y(near[2][half:])]

    def rows_of(near, corner):
        return jnp.concatenate(near + corner)

    def split(own_out, crossed):
        both = own_out.astype(f32) + crossed.astype(f32)
        mine, to_y, to_x = (both[i * tok_count : (i + 1) * tok_count] for i in range(3))
        last = both[3 * tok_count :].astype(bf16)
        return mine, to_y, to_x, swap_x(last[:half]), swap_y(last[half:])

    def pass_on(parts):
        mine, to_y, to_x, from_x, from_y = parts
        to_y = to_y.at[:half].add(from_x.astype(f32)).astype(bf16)
        to_x = to_x.at[half:].add(from_y.astype(f32)).astype(bf16)
        return mine, swap_y(to_y), swap_x(to_x)

    def turn_back_y(own_out, crossed):
        both = own_out.astype(f32) + crossed.astype(f32)
        mine, to_y, to_x, last = (both[i * tok_count : (i + 1) * tok_count] for i in range(4))
        return mine, to_x, swap_y(jnp.concatenate([to_y, last]).astype(bf16))

    def finish(slot, flow):
        plane = flow[0]
        for arrived in flow[1:]:
            plane = plane + arrived.astype(f32)
        return turn_z(plane.astype(bf16), -slot) if slot else plane

    state = {"ring1": turn_z(normed, 1), "near0": neighbours(normed)}

    wide, narrow = (0, 1), (1,)

    def act(name, slot, *operands):
        key = f"{name}{slot}"
        if name == "ring":
            state[key] = turn_z(*operands, 1)
        elif name == "near":
            state[key] = neighbours(*operands)
        elif name == "corner":
            state[key] = corners(*operands)
        elif name == "y":
            state[key] = swap_y(*operands)
        elif name == "x":
            state[key] = swap_x(jnp.concatenate(operands))
        elif name == "own":
            state[key] = rows_of(*operands) if slot in wide else jnp.concatenate(operands)
            state[f"other{slot}"] = swap_core(state[key])
        elif name == "cross":
            state[key] = swap_core(*operands)
        elif name == "parts":
            state[key] = split(*operands)
        elif name == "back_y":
            state[key] = turn_back_y(*operands)
        elif name == "back_x":
            mine, to_x, arrived = operands[0]
            mine = mine + arrived[:tok_count].astype(f32)
            state[key] = mine, swap_x((to_x + arrived[tok_count:].astype(f32)).astype(bf16))
        elif name == "flow":
            state[key] = pass_on(*operands)
        elif name == "plane":
            state[key] = finish(slot, *operands)

    needs = {
        "ring": lambda k: [f"ring{k - 1}"],
        "near": lambda k: [f"ring{k}"],
        "corner": lambda k: [f"near{k}"],
        "y": lambda k: [f"ring{k}"],
        "x": lambda k: [f"ring{k}", f"y{k}"],
        "own": lambda k: [f"near{k}", f"corner{k}"] if k in wide else [f"ring{k}", f"y{k}", f"x{k}"],
        "cross": lambda k: [f"other_out{k}"],
        "parts": lambda k: [f"own_out{k}", f"cross{k}"],
        "flow": lambda k: [f"parts{k}"],
        "back_y": lambda k: [f"own_out{k}", f"cross{k}"],
        "back_x": lambda k: [f"back_y{k}"],
        "plane": lambda k: [f"back_x{k}"] if k in narrow else [f"flow{k}"],
    }
    steps = [
        None, None, ("own", 0), None,
        ("own", 1), ("other", 1), ("own", 2), ("other", 2),
        ("own", 3), ("other", 3), ("other", 0),
        None, None, None, None,
    ]
    events = [
        [],
        [("corner", 0), ("near", 1), ("ring", 2)],
        [("own", 0)],
        [("corner", 1), ("y", 2), ("ring", 3)],
        [("own", 1), ("x", 2)],
        [("y", 3)],
        [("own", 2), ("cross", 1), ("x", 3)],
        [("back_y", 1)],
        [("own", 3), ("cross", 2)],
        [("parts", 2), ("back_x", 1)],
        [("cross", 3), ("flow", 2), ("plane", 1)],
        [("parts", 3), ("cross", 0), ("plane", 2)],
        [("flow", 3), ("parts", 0)],
        [("plane", 3), ("flow", 0)],
        [("plane", 0)],
    ]
    due = {1: ["ring1"], 12: ["plane1"], 14: ["plane2"]}
    for number, step in enumerate(steps):
        if number:
            keys = {key for name, slot in events[number] for key in needs[name](slot)}
            keys |= set(due.get(number, []))
            if steps[number - 1]:
                keys.add("{}_out{}".format(*steps[number - 1]))
            if step:
                keys.add("{}{}".format(*step))
            keys = sorted(keys & set(state))
            state.update(zip(keys, lax.optimization_barrier([state[key] for key in keys])))
        for name, slot in events[number]:
            act(name, slot, *(state[key] for key in needs[name](slot)))
        if step:
            which, k = step
            state[f"{which}_out{k}"] = gated_ffn(
                state[f"{which}{k}"], gate_of(k, int(which == "other")), w_in, w_out
            )
    total = hidden_f
    for k in range(4):
        total = total + state[f"plane{k}"].astype(f32)
    return total


def on_device(frames, queries, keys, values, expert_ids, gate_weights, w_in, w_out):
    attended = attention(queries[0], keys[0], values[0]).astype(jnp.float32)
    hidden_state = (frames[0].astype(jnp.float32) + attended).astype(jnp.bfloat16)
    hidden_f = hidden_state.astype(jnp.float32)
    normed = (
        hidden_f * lax.rsqrt(jnp.mean(hidden_f * hidden_f, axis=-1, keepdims=True) + EPSILON)
    ).astype(jnp.bfloat16)
    dense = lax.axis_size("ctx") == 8 and lax.axis_size("exp") == 4
    ffn = dense_sum if dense else routed_ffn
    layer_out = ffn(hidden_f, normed, expert_ids, gate_weights, w_in, w_out)
    return layer_out.astype(jnp.bfloat16)[None]


def solution(mesh):
    rows = P("exp", "ctx", None)
    in_specs = (rows,) * 6 + (P("exp", None, "ctx"), P("exp", "ctx", None))
    return jax.shard_map(
        on_device, mesh=mesh, in_specs=in_specs, out_specs=rows, check_vma=False
    )
```

```python
import functools
import math

import jax
import jax.numpy as jnp
from jax import lax
from jax.experimental import pallas as pl
from jax.experimental.pallas import tpu as pltpu
from jax.sharding import PartitionSpec as P

HEADS = 16
HD = 128


EPSILON = 1e-05


def gelu_tanh(values_in):
    return jax.nn.gelu(values_in, approximate=True)


def expert_partial(gathered, live_flags, first_w, second_w):
    total_rows = gathered.shape[0]
    out_width = second_w.shape[1]
    padded_rows = -(-total_rows // 128) * 128
    position = jnp.cumsum(live_flags) - 1
    live_count = jnp.sum(live_flags)
    target = jnp.where(live_flags > 0, position, padded_rows)
    order_idx = (
        jnp.zeros((padded_rows,), jnp.int32)
        .at[target]
        .set(jnp.arange(total_rows, dtype=jnp.int32), mode="drop")
    )
    block_count = (live_count + 127) // 128

    def one_block(block_num, packed):
        picked = lax.dynamic_slice_in_dim(order_idx, block_num * 128, 128)
        inputs = jnp.take(gathered, picked, axis=0)
        inner_act = gelu_tanh(jnp.dot(inputs, first_w, preferred_element_type=jnp.float32)).astype(
            jnp.bfloat16
        )
        output = jnp.dot(inner_act, second_w, preferred_element_type=jnp.float32).astype(
            jnp.bfloat16
        )
        return lax.dynamic_update_slice_in_dim(packed, output, block_num * 128, 0)

    packed = lax.fori_loop(
        0, block_count, one_block, jnp.zeros((padded_rows, out_width), jnp.bfloat16)
    )
    back_idx = jnp.where(live_flags > 0, position, 0).astype(jnp.int32)
    unpacked = jnp.take(packed, back_idx, axis=0)
    return jnp.where((live_flags > 0)[:, None], unpacked, jnp.zeros_like(unpacked))


def routed_ffn(hidden_f, normed, expert_ids, gate_weights, w_in, w_out):
    tok_count, model_width = normed.shape
    slot_ids = expert_ids[0].reshape(-1)
    slot_count = slot_ids.shape[0]
    exp_local = w_in.shape[0]
    num_experts = exp_local * lax.axis_size("exp")
    capacity = 2 * (slot_count // num_experts)
    onehot = (slot_ids[:, None] == jnp.arange(num_experts, dtype=jnp.int32)[None, :]).astype(
        jnp.int32
    )
    slot_rank = jnp.sum((jnp.cumsum(onehot, axis=0) - onehot) * onehot, axis=1)
    target = slot_ids * capacity + slot_rank
    send_matrix = (
        jnp.arange(num_experts * capacity, dtype=jnp.int32)[:, None] == target[None, :]
    ).astype(jnp.int32)
    token_matrix = send_matrix.reshape(num_experts * capacity, tok_count, 2).sum(-1)
    outgoing = jnp.dot(
        token_matrix.astype(jnp.bfloat16), normed, preferred_element_type=jnp.float32
    ).astype(jnp.bfloat16)
    outgoing = outgoing.reshape(num_experts, capacity, model_width)
    occupied = jnp.sum(send_matrix, axis=1).reshape(num_experts, capacity)
    arrived, arrived_flags = (
        lax.all_to_all(outgoing, "exp", split_axis=0, concat_axis=1, tiled=True),
        lax.all_to_all(occupied, "exp", split_axis=0, concat_axis=1, tiled=True),
    )
    gathered, gathered_flags = (
        lax.all_gather(arrived, "ctx", axis=1, tiled=True),
        lax.all_gather(arrived_flags, "ctx", axis=1, tiled=True),
    )
    summed_list = []
    for local_num in range(exp_local):
        partial_value = expert_partial(
            gathered[local_num], gathered_flags[local_num], w_in[local_num], w_out[local_num]
        )
        summed_list.append(
            lax.psum_scatter(partial_value, "ctx", scatter_dimension=0, tiled=True)
            .astype(jnp.float32)
            .astype(jnp.bfloat16)
        )
    summed = jnp.stack(summed_list)
    returned = lax.all_to_all(summed, "exp", split_axis=1, concat_axis=0, tiled=True)
    slot_out = jnp.dot(
        send_matrix.T.astype(jnp.bfloat16),
        returned.reshape(num_experts * capacity, model_width),
        preferred_element_type=jnp.float32,
    )
    tok_out = slot_out.reshape(tok_count, 2, model_width)
    gates = gate_weights[0]
    return hidden_f + gates[:, 0:1] * tok_out[:, 0] + gates[:, 1:2] * tok_out[:, 1]


def attend_kernel(q_ref, k_ref, v_ref, o_ref):
    scores = lax.dot_general(
        q_ref[...], k_ref[...], (((1,), (1,)), ((), ())), preferred_element_type=jnp.float32
    ) * (1.0 / math.sqrt(HD))
    raw = jnp.exp(scores - jnp.max(scores, axis=-1, keepdims=True))
    total = jnp.sum(raw, axis=-1, keepdims=True)
    mixed = jnp.dot(raw.astype(jnp.bfloat16), v_ref[...], preferred_element_type=jnp.float32)
    o_ref[...] = (mixed / total).astype(o_ref.dtype)


def attend_heads(packed, local_heads):
    frames = packed.shape[0]
    rows = 256
    return pl.pallas_call(
        attend_kernel,
        grid=(local_heads, frames // rows),
        in_specs=[
            pl.BlockSpec((rows, HD), lambda h, i: (i, h)),
            pl.BlockSpec((frames, HD), lambda h, i: (0, local_heads + h)),
            pl.BlockSpec((frames, HD), lambda h, i: (0, 2 * local_heads + h)),
        ],
        out_specs=pl.BlockSpec((rows, HD), lambda h, i: (i, h)),
        out_shape=jax.ShapeDtypeStruct((frames, local_heads * HD), jnp.bfloat16),
        compiler_params=pltpu.CompilerParams(vmem_limit_bytes=24 << 20),
        cost_estimate=pl.CostEstimate(
            flops=4 * local_heads * frames * frames * HD,
            bytes_accessed=8 * frames * local_heads * HD,
            transcendentals=local_heads * frames * frames,
        ),
        name="attend_heads",
    )(packed, packed, packed)


def attention(queries, keys, values):
    n_ctx = lax.axis_size("ctx")
    tok_count, width = queries.shape
    local_heads = HEADS // n_ctx
    piece = width // n_ctx
    outgoing = jnp.concatenate(
        [jnp.transpose(a.reshape(tok_count, n_ctx, piece), (1, 0, 2)) for a in (queries, keys, values)],
        axis=-1,
    )
    arrived = lax.all_to_all(outgoing, "ctx", split_axis=0, concat_axis=0, tiled=True)
    mixed = attend_heads(arrived.reshape(n_ctx * tok_count, 3 * piece), local_heads)
    returned = lax.all_to_all(
        mixed.reshape(n_ctx, tok_count, piece), "ctx", split_axis=0, concat_axis=0, tiled=True
    )
    return jnp.transpose(returned, (1, 0, 2)).reshape(tok_count, width)


def swap_core(a):
    return lax.ppermute(a, "exp", [(i, i ^ 1) for i in range(4)])


def swap_x(a):
    return lax.ppermute(a, "exp", [(i, i ^ 2) for i in range(4)])


def swap_y(a):
    return lax.ppermute(a, "ctx", [(i, i ^ 1) for i in range(8)])


def turn_z(a, steps):
    return lax.ppermute(a, "ctx", [(i, (i + 2 * steps) % 8) for i in range(8)])


def ffn_kernel(rows_ref, gate_ref, first_ref, second_ref, out_ref, act_ref):
    n_exp, width, inner = first_ref.shape
    cut = 512
    per = inner // cut
    gates = gate_ref[...].T

    @pl.loop(0, n_exp * per)
    def _(i):
        e, j = i // per, i % per
        cols = pl.ds(pl.multiple_of(j * cut, cut), cut)
        factor = gates[:, 0:1]
        for k in range(1, n_exp):
            factor = jnp.where(e == k, gates[:, k : k + 1], factor)
        act = gelu_tanh(
            jnp.dot(rows_ref[...], first_ref[e, :, cols], preferred_element_type=jnp.float32)
        )
        spot = pl.ds(pl.multiple_of(i * cut, cut), cut)
        act_ref[:, spot] = (act * factor).astype(act_ref.dtype)

    @pl.loop(0, width // cut)
    def _(i):
        cols = pl.ds(pl.multiple_of(i * cut, cut), cut)
        out_ref[:, cols] = jnp.dot(
            act_ref[...], second_ref[:, cols], preferred_element_type=jnp.float32
        ).astype(out_ref.dtype)


def gated_ffn(rows, gate, first_w, second_w):
    count, width = rows.shape
    n_exp, hidden = gate.shape[0], second_w.shape[0]
    vmem = pl.BlockSpec(memory_space=pltpu.VMEM)
    return pl.pallas_call(
        ffn_kernel,
        in_specs=[vmem] * 4,
        out_specs=vmem,
        out_shape=jax.ShapeDtypeStruct((count, width), jnp.bfloat16),
        scratch_shapes=[pltpu.VMEM((count, hidden), jnp.bfloat16)],
        compiler_params=pltpu.CompilerParams(vmem_limit_bytes=24 << 20),
        cost_estimate=pl.CostEstimate(
            flops=4 * count * width * hidden,
            bytes_accessed=4 * count * width,
            transcendentals=count * hidden,
        ),
        name="gated_ffn",
    )(rows, jnp.pad(gate, ((0, -n_exp % 8), (0, 0))), first_w, second_w)


def dense_sum(hidden_f, normed, expert_ids, gate_weights, w_in, w_out):
    tok_count, _ = normed.shape
    half = tok_count // 2
    n_local = w_in.shape[0]
    first_w, second_w = w_in, w_out
    f32, bf16 = jnp.float32, jnp.bfloat16
    small = jnp.concatenate([expert_ids[0].astype(f32).T, gate_weights[0].T], axis=0)
    small = jnp.stack([small, swap_y(small)])
    small = jnp.concatenate([small, swap_x(small)])
    small = jnp.stack([small, swap_core(small)])
    small = [small] + [turn_z(small, k) for k in range(1, 4)]
    local_ids = (
        lax.axis_index("exp") * n_local + jnp.arange(n_local, dtype=jnp.int32)
    ).astype(f32)

    def gate_of(slot, core):
        picked = small[slot][core]
        ids = jnp.transpose(picked[:, 0:2], (1, 0, 2)).reshape(2, -1)
        gates = jnp.transpose(picked[:, 2:4], (1, 0, 2)).reshape(2, -1)
        return jnp.sum(
            jnp.where(ids[None] == local_ids[:, None, None], gates[None], 0.0), axis=1
        )

    def neighbours(rows):
        return [rows, swap_y(rows), swap_x(rows)]

    def corners(near):
        return [swap_x(near[1][:half]), swap_y(near[2][half:])]

    def rows_of(near, corner):
        return jnp.concatenate(near + corner)

    def split(own_out, crossed):
        both = own_out.astype(f32) + crossed.astype(f32)
        mine, to_y, to_x = (both[i * tok_count : (i + 1) * tok_count] for i in range(3))
        last = both[3 * tok_count :].astype(bf16)
        return mine, to_y, to_x, swap_x(last[:half]), swap_y(last[half:])

    def pass_on(parts):
        mine, to_y, to_x, from_x, from_y = parts
        to_y = to_y.at[:half].add(from_x.astype(f32)).astype(bf16)
        to_x = to_x.at[half:].add(from_y.astype(f32)).astype(bf16)
        return mine, swap_y(to_y), swap_x(to_x)

    def turn_back_y(own_out, crossed):
        both = own_out.astype(f32) + crossed.astype(f32)
        mine, to_y, to_x, last = (both[i * tok_count : (i + 1) * tok_count] for i in range(4))
        return mine, to_x, swap_y(jnp.concatenate([to_y, last]).astype(bf16))

    def finish(slot, flow):
        plane = flow[0]
        for arrived in flow[1:]:
            plane = plane + arrived.astype(f32)
        return turn_z(plane.astype(bf16), -slot) if slot else plane

    state = {"ring1": turn_z(normed, 1), "near0": neighbours(normed)}

    wide, narrow = (0, 1), ()

    def act(name, slot, *operands):
        key = f"{name}{slot}"
        if name == "ring":
            state[key] = turn_z(*operands, 1)
        elif name == "near":
            state[key] = neighbours(*operands)
        elif name == "corner":
            state[key] = corners(*operands)
        elif name == "y":
            state[key] = swap_y(*operands)
        elif name == "x":
            state[key] = swap_x(jnp.concatenate(operands))
        elif name == "own":
            state[key] = rows_of(*operands) if slot in wide else jnp.concatenate(operands)
            state[f"other{slot}"] = swap_core(state[key])
        elif name == "cross":
            state[key] = swap_core(*operands)
        elif name == "parts":
            state[key] = split(*operands)
        elif name == "back_y":
            state[key] = turn_back_y(*operands)
        elif name == "back_x":
            mine, to_x, arrived = operands[0]
            mine = mine + arrived[:tok_count].astype(f32)
            state[key] = mine, swap_x((to_x + arrived[tok_count:].astype(f32)).astype(bf16))
        elif name == "flow":
            state[key] = pass_on(*operands)
        elif name == "plane":
            state[key] = finish(slot, *operands)

    needs = {
        "ring": lambda k: [f"ring{k - 1}"],
        "near": lambda k: [f"ring{k}"],
        "corner": lambda k: [f"near{k}"],
        "y": lambda k: [f"ring{k}"],
        "x": lambda k: [f"ring{k}", f"y{k}"],
        "own": lambda k: [f"near{k}", f"corner{k}"] if k in wide else [f"ring{k}", f"y{k}", f"x{k}"],
        "cross": lambda k: [f"other_out{k}"],
        "parts": lambda k: [f"own_out{k}", f"cross{k}"],
        "flow": lambda k: [f"parts{k}"],
        "back_y": lambda k: [f"own_out{k}", f"cross{k}"],
        "back_x": lambda k: [f"back_y{k}"],
        "plane": lambda k: [f"back_x{k}"] if k in narrow else [f"flow{k}"],
    }
    steps = [
        None, None, ("own", 0), None,
        ("own", 1), ("other", 1), ("own", 2), ("other", 2),
        ("own", 3), ("other", 3), ("other", 0),
        None, None, None, None,
    ]
    events = [
        [],
        [("corner", 0), ("near", 1), ("ring", 2)],
        [("own", 0)],
        [("corner", 1), ("y", 2), ("ring", 3)],
        [("own", 1), ("x", 2)],
        [("y", 3)],
        [("own", 2), ("cross", 1), ("x", 3)],
        [("parts", 1)],
        [("own", 3), ("cross", 2), ("flow", 1)],
        [("parts", 2), ("plane", 1)],
        [("cross", 3), ("flow", 2)],
        [("parts", 3), ("cross", 0), ("plane", 2)],
        [("flow", 3), ("parts", 0)],
        [("plane", 3), ("flow", 0)],
        [("plane", 0)],
    ]
    due = {1: ["ring1"], 11: ["plane1"], 14: ["plane2"]}
    for number, step in enumerate(steps):
        if number:
            keys = {key for name, slot in events[number] for key in needs[name](slot)}
            keys |= set(due.get(number, []))
            if steps[number - 1]:
                keys.add("{}_out{}".format(*steps[number - 1]))
            if step:
                keys.add("{}{}".format(*step))
            keys = sorted(keys & set(state))
            state.update(zip(keys, lax.optimization_barrier([state[key] for key in keys])))
        for name, slot in events[number]:
            act(name, slot, *(state[key] for key in needs[name](slot)))
        if step:
            which, k = step
            state[f"{which}_out{k}"] = gated_ffn(
                state[f"{which}{k}"], gate_of(k, int(which == "other")), first_w, second_w
            )
    total = hidden_f
    for k in range(4):
        total = total + state[f"plane{k}"].astype(f32)
    return total


def on_device(frames, queries, keys, values, expert_ids, gate_weights, w_in, w_out):
    dense = lax.axis_size("ctx") == 8 and lax.axis_size("exp") == 4
    if dense:
        w_in = pltpu.with_memory_space_constraint(w_in, pltpu.VMEM)
        w_out = pltpu.with_memory_space_constraint(
            w_out.reshape(-1, w_out.shape[-1]), pltpu.VMEM
        )
    attended = attention(queries[0], keys[0], values[0])
    attended = attended.astype(jnp.float32)
    hidden_state = (frames[0].astype(jnp.float32) + attended).astype(jnp.bfloat16)
    hidden_f = hidden_state.astype(jnp.float32)
    normed = (
        hidden_f * lax.rsqrt(jnp.mean(hidden_f * hidden_f, axis=-1, keepdims=True) + EPSILON)
    ).astype(jnp.bfloat16)
    ffn = dense_sum if dense else routed_ffn
    layer_out = ffn(hidden_f, normed, expert_ids, gate_weights, w_in, w_out)
    return layer_out.astype(jnp.bfloat16)[None]


def solution(mesh):
    rows = P("exp", "ctx", None)
    in_specs = (rows,) * 6 + (P("exp", None, "ctx"), P("exp", "ctx", None))
    return jax.shard_map(
        on_device, mesh=mesh, in_specs=in_specs, out_specs=rows, check_vma=False
    )
```

```python
import functools
import math

import jax
import jax.numpy as jnp
from jax import lax
from jax.experimental import pallas as pl
from jax.experimental.pallas import tpu as pltpu
from jax.sharding import PartitionSpec as P

HEADS = 16
HD = 128


EPSILON = 1e-05


def gelu_tanh(values_in):
    return jax.nn.gelu(values_in, approximate=True)


def expert_partial(gathered, live_flags, first_w, second_w):
    total_rows = gathered.shape[0]
    out_width = second_w.shape[1]
    padded_rows = -(-total_rows // 128) * 128
    position = jnp.cumsum(live_flags) - 1
    live_count = jnp.sum(live_flags)
    target = jnp.where(live_flags > 0, position, padded_rows)
    order_idx = (
        jnp.zeros((padded_rows,), jnp.int32)
        .at[target]
        .set(jnp.arange(total_rows, dtype=jnp.int32), mode="drop")
    )
    block_count = (live_count + 127) // 128

    def one_block(block_num, packed):
        picked = lax.dynamic_slice_in_dim(order_idx, block_num * 128, 128)
        inputs = jnp.take(gathered, picked, axis=0)
        inner_act = gelu_tanh(jnp.dot(inputs, first_w, preferred_element_type=jnp.float32)).astype(
            jnp.bfloat16
        )
        output = jnp.dot(inner_act, second_w, preferred_element_type=jnp.float32).astype(
            jnp.bfloat16
        )
        return lax.dynamic_update_slice_in_dim(packed, output, block_num * 128, 0)

    packed = lax.fori_loop(
        0, block_count, one_block, jnp.zeros((padded_rows, out_width), jnp.bfloat16)
    )
    back_idx = jnp.where(live_flags > 0, position, 0).astype(jnp.int32)
    unpacked = jnp.take(packed, back_idx, axis=0)
    return jnp.where((live_flags > 0)[:, None], unpacked, jnp.zeros_like(unpacked))


def routed_ffn(hidden_f, normed, expert_ids, gate_weights, w_in, w_out):
    tok_count, model_width = normed.shape
    slot_ids = expert_ids[0].reshape(-1)
    slot_count = slot_ids.shape[0]
    exp_local = w_in.shape[0]
    num_experts = exp_local * lax.axis_size("exp")
    capacity = 2 * (slot_count // num_experts)
    onehot = (slot_ids[:, None] == jnp.arange(num_experts, dtype=jnp.int32)[None, :]).astype(
        jnp.int32
    )
    slot_rank = jnp.sum((jnp.cumsum(onehot, axis=0) - onehot) * onehot, axis=1)
    target = slot_ids * capacity + slot_rank
    send_matrix = (
        jnp.arange(num_experts * capacity, dtype=jnp.int32)[:, None] == target[None, :]
    ).astype(jnp.int32)
    token_matrix = send_matrix.reshape(num_experts * capacity, tok_count, 2).sum(-1)
    outgoing = jnp.dot(
        token_matrix.astype(jnp.bfloat16), normed, preferred_element_type=jnp.float32
    ).astype(jnp.bfloat16)
    outgoing = outgoing.reshape(num_experts, capacity, model_width)
    occupied = jnp.sum(send_matrix, axis=1).reshape(num_experts, capacity)
    arrived, arrived_flags = (
        lax.all_to_all(outgoing, "exp", split_axis=0, concat_axis=1, tiled=True),
        lax.all_to_all(occupied, "exp", split_axis=0, concat_axis=1, tiled=True),
    )
    gathered, gathered_flags = (
        lax.all_gather(arrived, "ctx", axis=1, tiled=True),
        lax.all_gather(arrived_flags, "ctx", axis=1, tiled=True),
    )
    summed_list = []
    for local_num in range(exp_local):
        partial_value = expert_partial(
            gathered[local_num], gathered_flags[local_num], w_in[local_num], w_out[local_num]
        )
        summed_list.append(
            lax.psum_scatter(partial_value, "ctx", scatter_dimension=0, tiled=True)
            .astype(jnp.float32)
            .astype(jnp.bfloat16)
        )
    summed = jnp.stack(summed_list)
    returned = lax.all_to_all(summed, "exp", split_axis=1, concat_axis=0, tiled=True)
    slot_out = jnp.dot(
        send_matrix.T.astype(jnp.bfloat16),
        returned.reshape(num_experts * capacity, model_width),
        preferred_element_type=jnp.float32,
    )
    tok_out = slot_out.reshape(tok_count, 2, model_width)
    gates = gate_weights[0]
    return hidden_f + gates[:, 0:1] * tok_out[:, 0] + gates[:, 1:2] * tok_out[:, 1]


def attend_kernel(q_ref, k_ref, v_ref, o_ref):
    scores = lax.dot_general(
        q_ref[...], k_ref[...], (((1,), (1,)), ((), ())), preferred_element_type=jnp.float32
    ) * (1.0 / math.sqrt(HD))
    raw = jnp.exp(scores - jnp.max(scores, axis=-1, keepdims=True))
    total = jnp.sum(raw, axis=-1, keepdims=True)
    mixed = jnp.dot(raw.astype(jnp.bfloat16), v_ref[...], preferred_element_type=jnp.float32)
    o_ref[...] = (mixed / total).astype(o_ref.dtype)


def attend_heads(packed, local_heads):
    frames = packed.shape[0]
    rows = 256
    return pl.pallas_call(
        attend_kernel,
        grid=(local_heads, frames // rows),
        in_specs=[
            pl.BlockSpec((rows, HD), lambda h, i: (i, h)),
            pl.BlockSpec((frames, HD), lambda h, i: (0, local_heads + h)),
            pl.BlockSpec((frames, HD), lambda h, i: (0, 2 * local_heads + h)),
        ],
        out_specs=pl.BlockSpec((rows, HD), lambda h, i: (i, h)),
        out_shape=jax.ShapeDtypeStruct((frames, local_heads * HD), jnp.bfloat16),
        compiler_params=pltpu.CompilerParams(vmem_limit_bytes=24 << 20),
        cost_estimate=pl.CostEstimate(
            flops=4 * local_heads * frames * frames * HD,
            bytes_accessed=8 * frames * local_heads * HD,
            transcendentals=local_heads * frames * frames,
        ),
        name="attend_heads",
    )(packed, packed, packed)


def attention(queries, keys, values):
    n_ctx = lax.axis_size("ctx")
    tok_count, width = queries.shape
    local_heads = HEADS // n_ctx
    piece = width // n_ctx
    outgoing = jnp.concatenate(
        [jnp.transpose(a.reshape(tok_count, n_ctx, piece), (1, 0, 2)) for a in (queries, keys, values)],
        axis=-1,
    )
    arrived = lax.all_to_all(outgoing, "ctx", split_axis=0, concat_axis=0, tiled=True)
    mixed = attend_heads(arrived.reshape(n_ctx * tok_count, 3 * piece), local_heads)
    returned = lax.all_to_all(
        mixed.reshape(n_ctx, tok_count, piece), "ctx", split_axis=0, concat_axis=0, tiled=True
    )
    return jnp.transpose(returned, (1, 0, 2)).reshape(tok_count, width)


def swap_core(a):
    return lax.ppermute(a, "exp", [(i, i ^ 1) for i in range(4)])


def swap_x(a):
    return lax.ppermute(a, "exp", [(i, i ^ 2) for i in range(4)])


def swap_y(a):
    return lax.ppermute(a, "ctx", [(i, i ^ 1) for i in range(8)])


def turn_z(a, steps):
    return lax.ppermute(a, "ctx", [(i, (i + 2 * steps) % 8) for i in range(8)])


def ffn_kernel(rows_ref, gate_ref, first_ref, second_ref, out_ref, act_ref):
    n_exp, width, inner = first_ref.shape
    cut = 1024
    per = inner // cut
    gates = gate_ref[...].T

    @pl.loop(0, n_exp * per)
    def _(i):
        e, j = i // per, i % per
        cols = pl.ds(pl.multiple_of(j * cut, cut), cut)
        factor = gates[:, 0:1]
        for k in range(1, n_exp):
            factor = jnp.where(e == k, gates[:, k : k + 1], factor)
        act = gelu_tanh(
            jnp.dot(rows_ref[...], first_ref[e, :, cols], preferred_element_type=jnp.float32)
        )
        spot = pl.ds(pl.multiple_of(i * cut, cut), cut)
        act_ref[:, spot] = (act * factor).astype(act_ref.dtype)

    @pl.loop(0, width // cut)
    def _(i):
        cols = pl.ds(pl.multiple_of(i * cut, cut), cut)
        out_ref[:, cols] = jnp.dot(
            act_ref[...], second_ref[:, cols], preferred_element_type=jnp.float32
        ).astype(out_ref.dtype)


def gated_ffn(rows, gate, first_w, second_w):
    count, width = rows.shape
    n_exp, hidden = gate.shape[0], second_w.shape[0]
    vmem = pl.BlockSpec(memory_space=pltpu.VMEM)
    return pl.pallas_call(
        ffn_kernel,
        in_specs=[vmem] * 4,
        out_specs=vmem,
        out_shape=jax.ShapeDtypeStruct((count, width), jnp.bfloat16),
        scratch_shapes=[pltpu.VMEM((count, hidden), jnp.bfloat16)],
        compiler_params=pltpu.CompilerParams(vmem_limit_bytes=24 << 20),
        cost_estimate=pl.CostEstimate(
            flops=4 * count * width * hidden,
            bytes_accessed=4 * count * width,
            transcendentals=count * hidden,
        ),
        name="gated_ffn",
    )(rows, jnp.pad(gate, ((0, -n_exp % 8), (0, 0))), first_w, second_w)


def dense_sum(hidden_f, normed, expert_ids, gate_weights, w_in, w_out):
    tok_count, _ = normed.shape
    half = tok_count // 2
    n_local = w_in.shape[0]
    first_w, second_w = w_in, w_out
    f32, bf16 = jnp.float32, jnp.bfloat16
    small = jnp.concatenate([expert_ids[0].astype(f32).T, gate_weights[0].T], axis=0)
    small = jnp.stack([small, swap_y(small)])
    small = jnp.concatenate([small, swap_x(small)])
    small = jnp.stack([small, swap_core(small)])
    small = [small] + [turn_z(small, k) for k in range(1, 4)]
    local_ids = (
        lax.axis_index("exp") * n_local + jnp.arange(n_local, dtype=jnp.int32)
    ).astype(f32)

    def gate_of(slot, core):
        picked = small[slot][core]
        ids = jnp.transpose(picked[:, 0:2], (1, 0, 2)).reshape(2, -1)
        gates = jnp.transpose(picked[:, 2:4], (1, 0, 2)).reshape(2, -1)
        return jnp.sum(
            jnp.where(ids[None] == local_ids[:, None, None], gates[None], 0.0), axis=1
        )

    def neighbours(rows):
        return [rows, swap_y(rows), swap_x(rows)]

    def corners(near):
        return [swap_x(near[1][:half]), swap_y(near[2][half:])]

    def rows_of(near, corner):
        return jnp.concatenate(near + corner)

    def split(own_out, crossed):
        both = own_out.astype(f32) + crossed.astype(f32)
        mine, to_y, to_x = (both[i * tok_count : (i + 1) * tok_count] for i in range(3))
        last = both[3 * tok_count :].astype(bf16)
        return mine, to_y, to_x, swap_x(last[:half]), swap_y(last[half:])

    def pass_on(parts):
        mine, to_y, to_x, from_x, from_y = parts
        to_y = to_y.at[:half].add(from_x.astype(f32)).astype(bf16)
        to_x = to_x.at[half:].add(from_y.astype(f32)).astype(bf16)
        return mine, swap_y(to_y), swap_x(to_x)

    def turn_back_y(own_out, crossed):
        both = own_out.astype(f32) + crossed.astype(f32)
        mine, to_y, to_x, last = (both[i * tok_count : (i + 1) * tok_count] for i in range(4))
        return mine, to_x, swap_y(jnp.concatenate([to_y, last]).astype(bf16))

    def finish(slot, flow):
        plane = flow[0]
        for arrived in flow[1:]:
            plane = plane + arrived.astype(f32)
        return turn_z(plane.astype(bf16), -slot) if slot else plane

    state = {"ring1": turn_z(normed, 1), "near0": neighbours(normed)}

    wide, narrow = (0, 1), ()

    def act(name, slot, *operands):
        key = f"{name}{slot}"
        if name == "ring":
            state[key] = turn_z(*operands, 1)
        elif name == "near":
            state[key] = neighbours(*operands)
        elif name == "corner":
            state[key] = corners(*operands)
        elif name == "y":
            state[key] = swap_y(*operands)
        elif name == "x":
            state[key] = swap_x(jnp.concatenate(operands))
        elif name == "own":
            state[key] = rows_of(*operands) if slot in wide else jnp.concatenate(operands)
            state[f"other{slot}"] = swap_core(state[key])
        elif name == "cross":
            state[key] = swap_core(*operands)
        elif name == "parts":
            state[key] = split(*operands)
        elif name == "back_y":
            state[key] = turn_back_y(*operands)
        elif name == "back_x":
            mine, to_x, arrived = operands[0]
            mine = mine + arrived[:tok_count].astype(f32)
            state[key] = mine, swap_x((to_x + arrived[tok_count:].astype(f32)).astype(bf16))
        elif name == "flow":
            state[key] = pass_on(*operands)
        elif name == "plane":
            state[key] = finish(slot, *operands)

    needs = {
        "ring": lambda k: [f"ring{k - 1}"],
        "near": lambda k: [f"ring{k}"],
        "corner": lambda k: [f"near{k}"],
        "y": lambda k: [f"ring{k}"],
        "x": lambda k: [f"ring{k}", f"y{k}"],
        "own": lambda k: [f"near{k}", f"corner{k}"] if k in wide else [f"ring{k}", f"y{k}", f"x{k}"],
        "cross": lambda k: [f"other_out{k}"],
        "parts": lambda k: [f"own_out{k}", f"cross{k}"],
        "flow": lambda k: [f"parts{k}"],
        "back_y": lambda k: [f"own_out{k}", f"cross{k}"],
        "back_x": lambda k: [f"back_y{k}"],
        "plane": lambda k: [f"back_x{k}"] if k in narrow else [f"flow{k}"],
    }
    steps = [
        None, None, ("own", 0), None,
        ("own", 1), ("other", 1), ("own", 2), ("other", 2),
        ("own", 3), ("other", 3), ("other", 0),
        None, None, None, None,
    ]
    events = [
        [],
        [("corner", 0), ("near", 1), ("ring", 2)],
        [("own", 0)],
        [("corner", 1), ("y", 2), ("ring", 3)],
        [("own", 1), ("x", 2)],
        [("y", 3)],
        [("own", 2), ("cross", 1), ("x", 3)],
        [("parts", 1)],
        [("own", 3), ("cross", 2), ("flow", 1)],
        [("parts", 2), ("plane", 1)],
        [("cross", 3), ("flow", 2)],
        [("parts", 3), ("cross", 0), ("plane", 2)],
        [("flow", 3), ("parts", 0)],
        [("plane", 3), ("flow", 0)],
        [("plane", 0)],
    ]
    due = {1: ["ring1"], 11: ["plane1"], 14: ["plane2"]}
    for number, step in enumerate(steps):
        if number:
            keys = {key for name, slot in events[number] for key in needs[name](slot)}
            keys |= set(due.get(number, []))
            if steps[number - 1]:
                keys.add("{}_out{}".format(*steps[number - 1]))
            if step:
                keys.add("{}{}".format(*step))
            keys = sorted(keys & set(state))
            state.update(zip(keys, lax.optimization_barrier([state[key] for key in keys])))
        for name, slot in events[number]:
            act(name, slot, *(state[key] for key in needs[name](slot)))
        if step:
            which, k = step
            state[f"{which}_out{k}"] = gated_ffn(
                state[f"{which}{k}"], gate_of(k, int(which == "other")), first_w, second_w
            )
    total = hidden_f
    for k in range(4):
        total = total + state[f"plane{k}"].astype(f32)
    return total


def on_device(frames, queries, keys, values, expert_ids, gate_weights, w_in, w_out):
    dense = lax.axis_size("ctx") == 8 and lax.axis_size("exp") == 4
    if dense:
        w_in = pltpu.with_memory_space_constraint(w_in, pltpu.VMEM)
        w_out = pltpu.with_memory_space_constraint(
            w_out.reshape(-1, w_out.shape[-1]), pltpu.VMEM
        )
    attended = attention(queries[0], keys[0], values[0])
    attended = attended.astype(jnp.float32)
    hidden_state = (frames[0].astype(jnp.float32) + attended).astype(jnp.bfloat16)
    hidden_f = hidden_state.astype(jnp.float32)
    normed = (
        hidden_f * lax.rsqrt(jnp.mean(hidden_f * hidden_f, axis=-1, keepdims=True) + EPSILON)
    ).astype(jnp.bfloat16)
    ffn = dense_sum if dense else routed_ffn
    layer_out = ffn(hidden_f, normed, expert_ids, gate_weights, w_in, w_out)
    return layer_out.astype(jnp.bfloat16)[None]


def solution(mesh):
    rows = P("exp", "ctx", None)
    in_specs = (rows,) * 6 + (P("exp", None, "ctx"), P("exp", "ctx", None))
    return jax.shard_map(
        on_device, mesh=mesh, in_specs=in_specs, out_specs=rows, check_vma=False
    )
```
